128 devices in a mesh: ctx: 64 (over y, z, x), head: 2 (over core).
Axes of the slice: x: 4, y: 4, z: 4, core: 2. Of those that a mesh axis runs over, the one named last changes fastest.
Arguments:
- queries: float32 [32768, 1024], P('ctx', 'head'), may hold values from -5 to 5
- keys: float32 [32768, 1024], P('ctx', 'head'), may hold values from -5 to 5
- values: float32 [32768, 1024], P('ctx', 'head'), may hold values from -6 to 6
- transitions: float32 [32768, 1024], P('ctx', 'head'), may hold values from -6 to 6
- betas: float32 [8, 32768], P('head', 'ctx'), may hold values from 0 to 2
- documents: int32 [32768], P('ctx'), may hold values from 0 to 31, never falling along the last dimension, each value on 1 to 2048 neighbouring positions
- out_weight: float32 [1024, 2048], P('head'), may hold values from -1.5 to 1.5
Outputs:
- output: float32 [32768, 2048], P(('ctx', 'head'))
The draws below stay inside these ranges and needn't reach their ends.
Inputs may be any that keep to these rules, and one draw needn't show every extreme that they name: `documents`: document ids never fall along the tokens; every document holds at most 2048 tokens.
All inputs are finite; a program needn't handle non-finite values.
Results may differ from the reference program's by a relative error of at most 0.0003.
Values sent between devices are 32-bit elements; how exact they have to be, the bound alone decides.
A program may use at most 320 MiB of HBM per device.

```python
import math
import jax
import jax.numpy as jnp
import numpy as np
from jax import lax

D = 2048
HEADS = 8
DH = 128
BLOCK_TOKENS = 512
CONTEXT_TOKENS = 32768


def paired_rows(key):
    columns = HEADS * DH
    query_rows = jax.random.truncated_normal(jax.random.fold_in(key, 101), -5.0, 5.0, (CONTEXT_TOKENS, columns))
    key_rows = jax.random.truncated_normal(jax.random.fold_in(key, 102), -5.0, 5.0, (CONTEXT_TOKENS, columns))
    return (query_rows, key_rows)


def draw_queries(key, part):
    return paired_rows(key)[0]


def draw_keys(key, part):
    return paired_rows(key)[1]


def draw_betas(key, part):
    slow_share = 0.5
    slow_heads = jax.random.uniform(jax.random.fold_in(key, 201), (HEADS, 1)) < slow_share
    small_part = jnp.exp(jax.random.uniform(jax.random.fold_in(key, 202), (HEADS, CONTEXT_TOKENS), minval=math.log(0.001), maxval=math.log(0.04)))
    apply_reflection = jax.random.uniform(jax.random.fold_in(key, 203), (HEADS, CONTEXT_TOKENS)) < 0.5
    slow_beta = jnp.where(apply_reflection, 2.0 - small_part, small_part)
    fast_beta = jax.random.uniform(jax.random.fold_in(key, 204), (HEADS, CONTEXT_TOKENS), minval=0.3, maxval=1.7)
    strengths = jnp.where(slow_heads, slow_beta, fast_beta)
    segment_count = max(CONTEXT_TOKENS // (4 * BLOCK_TOKENS), 2)
    segment_starts = jax.random.randint(jax.random.fold_in(key, 205), (segment_count,), 0, CONTEXT_TOKENS)
    block_offsets = jnp.arange(CONTEXT_TOKENS)[None, :] - segment_starts[:, None]
    inside = jnp.any((block_offsets >= 0) & (block_offsets < 40), axis=0)
    return jnp.where(inside[None, :], 1.0, strengths)


def steps_of(stream_key, shape, cuts, low, largest):
    gain, own = 1.0, jax.random.fold_in(stream_key, 6)
    for position, blocks in cuts:
        draws = jnp.exp(jax.random.uniform(jax.random.fold_in(own, position), (blocks,), jnp.float32, low / len(cuts), largest / len(cuts)))
        gain = gain * jnp.repeat(draws, shape[position] // blocks).reshape([-1 if axis == position else 1 for axis in range(len(shape))])
    return gain


def split_up(number_of, total, most, skew):
    weights = [(1 << 20) // math.isqrt(standing ** skew) + 1 for standing in range(2, number_of + 1)]
    surplus, given = total - most - (number_of - 1), [1] * (number_of - 1)
    while surplus > 0:
        free = [i for i in range(number_of - 1) if given[i] < most]
        whole, left = sum([weights[i] for i in free]), surplus
        for i in free:
            extra = min(most - given[i], max(1, left * weights[i] // whole), surplus)
            given[i] = given[i] + extra
            surplus = surplus - extra
    return np.array([most] + given)


def uneven(key, amount, total, reach, slope):
    if amount == 2:
        one = jax.random.randint(key, (), max(1, total - reach), min(reach, total - 1) + 1)
        return jnp.stack([one, total - one])
    tallies = jnp.asarray(split_up(amount, total, reach, slope), jnp.int32)
    couples = (amount - 1) // 2
    giver, sink = tallies[1:1 + 2 * couples:2], tallies[2:2 + 2 * couples:2]
    room = jnp.minimum(giver - 1, reach - sink)
    moved = jax.random.randint(jax.random.fold_in(key, 1), (couples,), 0, 1 << 20) % (room + 1)
    tallies = tallies.at[1:1 + 2 * couples:2].set(giver - moved).at[2:2 + 2 * couples:2].set(sink + moved)
    return tallies[jax.random.permutation(jax.random.fold_in(key, 2), amount)]


def gaussian(stream_key, shape, width, bound, shards=(), kind=jnp.bfloat16):
    level = steps_of(stream_key, shape, shards, -0.22, 0.18) if shards else 1.0
    result = jax.random.normal(stream_key, shape, jnp.float32) * width * level
    return jnp.minimum(jnp.maximum(result, -bound), bound).astype(kind)


def setup_inputs(seed: int = 0) -> dict:
    seeds = jax.random.split(jax.random.key(seed), 8)
    return {
        "queries": draw_queries(jax.random.fold_in(seeds[7], 71), 0),
        "keys": draw_keys(jax.random.fold_in(seeds[7], 71), 0),
        "values": gaussian(seeds[2], (CONTEXT_TOKENS, HEADS * DH), 1.0, 6.0, ((0, 64), (1, 2)), jnp.float32),
        "transitions": gaussian(seeds[3], (CONTEXT_TOKENS, HEADS * DH), 1.0, 6.0, ((0, 64), (1, 2)), jnp.float32),
        "betas": draw_betas(jax.random.fold_in(seeds[7], 71), 0),
        "documents": jnp.searchsorted(jnp.cumsum(uneven(seeds[5], CONTEXT_TOKENS // (2 * BLOCK_TOKENS), CONTEXT_TOKENS, 4 * BLOCK_TOKENS, 1)), jnp.arange(CONTEXT_TOKENS), side="right").astype(jnp.int32),
        "out_weight": gaussian(seeds[6], (HEADS * DH, D), (max(HEADS * DH // 64, 1)) ** -0.5, 1.5, ((0, 2),), jnp.float32),
    }


HIGHEST = lax.Precision.HIGHEST

def contract(pattern, left_operand, right_operand):
    return jnp.einsum(pattern, left_operand, right_operand, precision=HIGHEST)

def piece_length(length):
    return 128 if length >= 256 else length // 2

def unit_lower_inverse(lower_mat):
    lead = lower_mat.shape[:-2]
    order = lower_mat.shape[-1]
    depth = len(lead)
    inverse_blocks = jnp.ones(lead + (order, 1, 1), jnp.float32)
    size = 1
    while size < order:
        count = order // (2 * size)
        tiled = lower_mat.reshape(lead + (count, 2, size, count, 2, size))
        diagonal_tiles = jnp.diagonal(tiled, axis1=depth, axis2=depth + 3)
        lower_left = jnp.moveaxis(diagonal_tiles[..., 1, :, 0, :, :], -1, depth)
        paired = inverse_blocks.reshape(lead + (count, 2, size, size))
        upper_inverse = paired[..., 0, :, :]
        lower_inverse = paired[..., 1, :, :]
        off_block = -contract('...ij,...jk->...ik', lower_inverse, contract('...ij,...jk->...ik', lower_left, upper_inverse))
        top_half = jnp.concatenate([upper_inverse, jnp.zeros_like(upper_inverse)], axis=-1)
        bottom_half = jnp.concatenate([off_block, lower_inverse], axis=-1)
        inverse_blocks = jnp.concatenate([top_half, bottom_half], axis=-2)
        size = size * 2
    return inverse_blocks.reshape(lead + (order, order))

def local_parts(queries, keys, transitions, betas):
    batches, length, groups, head_size = queries.shape
    piece_size = piece_length(length)
    pieces = length // piece_size
    sub_shape = (batches, pieces, piece_size, groups, head_size)
    unit_dirs = transitions * lax.rsqrt(lax.optimization_barrier(jnp.sum(transitions * transitions, axis=-1, keepdims=True)) + 1e-06)
    query_sub = queries.reshape(sub_shape)
    key_sub = keys.reshape(sub_shape)
    trans_sub = unit_dirs.reshape(sub_shape)
    beta_sub = jnp.transpose(betas.reshape(batches, pieces, piece_size, groups), (0, 1, 3, 2))
    row_ids = lax.broadcasted_iota(jnp.int32, (piece_size, piece_size), 0)
    col_ids = lax.broadcasted_iota(jnp.int32, (piece_size, piece_size), 1)
    strictly = row_ids > col_ids
    within = row_ids >= col_ids
    gram_matrix = contract('bnihd,bnjhd->bnhij', trans_sub, trans_sub)
    lower_mat = jnp.eye(piece_size, dtype=jnp.float32) + jnp.where(strictly, beta_sub[..., :, None] * gram_matrix, 0.0)
    beta_keys = jnp.where(strictly, beta_sub[..., :, None] * contract('bnihd,bnjhd->bnhij', trans_sub, key_sub), 0.0)
    beta_rows = beta_sub[..., None] * jnp.transpose(trans_sub, (0, 1, 3, 2, 4))
    inverse = unit_lower_inverse(lower_mat)
    solved = contract('bnhij,bnhjk->bnhik', inverse, jnp.concatenate([beta_keys, beta_rows], axis=-1))
    carried = solved[..., :piece_size]
    applied = solved[..., piece_size:]
    query_dirs = jnp.where(within, contract('bnihd,bnshd->bnhis', query_sub, trans_sub), 0.0)
    own_scores = contract('bnihd,bnjhd->bnhij', query_sub, key_sub) - contract('bnhis,bnhsj->bnhij', query_dirs, carried)
    query_hat = jnp.transpose(query_sub, (0, 1, 3, 2, 4)) - contract('bnhis,bnhsd->bnhid', query_dirs, applied)
    key_hat = jnp.transpose(key_sub, (0, 1, 3, 2, 4)) - contract('bnhsj,bnshd->bnhjd', carried, trans_sub)
    sub_steps = jnp.eye(head_size, dtype=jnp.float32) - contract('bnshe,bnhsf->bnhef', trans_sub, applied)
    return (query_hat, key_hat, own_scores, sub_steps)

def block_form(query_hat, key_hat, own_scores, sub_steps):
    batches, pieces, groups, piece_size, head_size = query_hat.shape
    rows_out = []
    queries_out = []
    for query_index in range(pieces):
        current = query_hat[:, query_index]
        tile_list = [own_scores[:, query_index]]
        for key_index in range(query_index - 1, -1, -1):
            tile_list.insert(0, contract('bhid,bhjd->bhij', current, key_hat[:, key_index]))
            current = contract('bhie,bhef->bhif', current, sub_steps[:, key_index])
        if query_index < pieces - 1:
            tile_list.append(jnp.zeros((batches, groups, piece_size, (pieces - 1 - query_index) * piece_size), jnp.float32))
        rows_out.append(jnp.concatenate(tile_list, axis=-1))
        queries_out.append(current)
    intra_scores = jnp.concatenate(rows_out, axis=2)
    block_queries = jnp.stack(queries_out, axis=2).reshape(batches, groups, pieces * piece_size, head_size)
    suffix = jnp.broadcast_to(jnp.eye(head_size, dtype=jnp.float32), (batches, groups, head_size, head_size))
    keys_out = [None] * pieces
    for key_index in range(pieces - 1, -1, -1):
        keys_out[key_index] = contract('bhef,bhjf->bhje', suffix, key_hat[:, key_index])
        suffix = contract('bhef,bhfg->bheg', suffix, sub_steps[:, key_index])
    block_keys = jnp.stack(keys_out, axis=2).reshape(batches, groups, pieces * piece_size, head_size)
    return (block_queries, block_keys, intra_scores, suffix)

def absorb(softmax_state, raw_scores, allowed, value_part):
    row_peak, row_total, summed = softmax_state
    masked = jnp.where(allowed, raw_scores, -jnp.inf)
    new_peak = jnp.maximum(row_peak, lax.optimization_barrier(jnp.max(masked, axis=-1, keepdims=True)))
    factor = jnp.exp(row_peak - new_peak)
    weights = jnp.where(allowed, jnp.exp(masked - new_peak), 0.0)
    row_total = row_total * factor + lax.optimization_barrier(jnp.sum(weights, axis=-1, keepdims=True))
    summed = summed * factor + contract('...ij,...jd->...id', weights, value_part)
    return (new_peak, row_total, summed)

def reference(queries, keys, values, transitions, betas, documents, out_weight):
    head_count = betas.shape[0]
    head_size = queries.shape[1] // head_count
    length = BLOCK_TOKENS
    total_blocks = queries.shape[0] // length
    query_tiles = queries.reshape(total_blocks, length, head_count, head_size)
    key_blocks = keys.reshape(total_blocks, length, head_count, head_size)
    trans_blocks = transitions.reshape(total_blocks, length, head_count, head_size)
    beta_blocks = jnp.transpose(betas.reshape(head_count, total_blocks, length), (1, 2, 0))
    value_blocks = jnp.transpose(values.reshape(total_blocks, length, head_count, head_size), (0, 2, 1, 3))
    document_blocks = documents.reshape(total_blocks, length)
    score_scale = 1.0 / math.sqrt(head_size)

    def prepare(sliced):
        parts = local_parts(sliced[0][None], sliced[1][None], sliced[2][None], sliced[3][None])
        formed = block_form(*parts)
        return (formed[1][0], formed[3][0])
    all_keys, all_steps = lax.map(prepare, (query_tiles, key_blocks, trans_blocks, beta_blocks))
    causal = lax.broadcasted_iota(jnp.int32, (length, length), 0) >= lax.broadcasted_iota(jnp.int32, (length, length), 1)

    def attend(block_index):

        def pick(array):
            return lax.dynamic_index_in_dim(array, block_index, 0, keepdims=True)
        parts = local_parts(pick(query_tiles), pick(key_blocks), pick(trans_blocks), pick(beta_blocks))
        formed = block_form(*parts)
        current = formed[0][0]
        doc_row = pick(document_blocks)[0]
        own_allowed = (doc_row[:, None] == doc_row[None, :]) & causal
        softmax_state = (jnp.full((head_count, length, 1), -jnp.inf, jnp.float32), jnp.zeros((head_count, length, 1), jnp.float32), jnp.zeros((head_count, length, head_size), jnp.float32))
        softmax_state = absorb(softmax_state, formed[2][0] * score_scale, own_allowed[None], pick(value_blocks)[0])
        for distance in range(1, 4):
            source = jnp.maximum(block_index - distance, 0).astype(jnp.int32)
            if distance > 1:
                middle = jnp.maximum(block_index - distance + 1, 0).astype(jnp.int32)
                current = contract('hie,hef->hif', current, all_steps[middle])
            valid_block = block_index - distance >= 0
            allowed = (doc_row[:, None] == document_blocks[source][None, :]) & valid_block
            raw_scores = contract('hid,hjd->hij', current, all_keys[source]) * score_scale
            softmax_state = absorb(softmax_state, raw_scores, allowed[None], value_blocks[source])
        attended = softmax_state[2] / softmax_state[1]
        return jnp.transpose(attended, (1, 0, 2)).reshape(length, head_count * head_size)
    attended = lax.map(attend, jnp.arange(total_blocks, dtype=jnp.int32)).reshape(total_blocks * length, head_count * head_size)
    return jnp.dot(attended, out_weight, precision=HIGHEST, preferred_element_type=jnp.float32)
```

```python
import functools
import math

import jax
import jax.numpy as jnp
from jax import lax
from jax.experimental import pallas as pl
from jax.experimental.pallas import tpu as pltpu
from jax.sharding import PartitionSpec as P

MESH = pl.DeviceIdType.MESH
HIGH = lax.Precision.HIGH
ROWS = 512
DH = 128
G = 4
PIECE = 128
PIECES = ROWS // PIECE
MASKED = -1e30


def dot(left, right, left_dim=1, right_dim=0):
    return lax.dot_general(
        left,
        right,
        (((left_dim,), (right_dim,)), ((), ())),
        precision=HIGH,
        preferred_element_type=jnp.float32,
    )


def iotas(rows, columns):
    return (
        lax.broadcasted_iota(jnp.int32, (rows, columns), 0),
        lax.broadcasted_iota(jnp.int32, (rows, columns), 1),
    )


def unit_lower_inverses(lowers):
    row, col = iotas(PIECE, PIECE)
    eye = jnp.where(row == col, 1.0, 0.0)

    def level_part(lower, bit):
        keep = ((row >> (bit + 1)) == (col >> (bit + 1))) & (((row >> bit) & 1) == 1) & (((col >> bit) & 1) == 0)
        return jnp.where(keep, lower, 0.0)

    inverses = [eye - level_part(lower, 0) for lower in lowers]
    for bit in range(1, 7):
        products = [dot(level_part(lower, bit), inverse) for lower, inverse in zip(lowers, inverses)]
        products = [dot(inverse, product) for inverse, product in zip(inverses, products)]
        inverses = [inverse - product for inverse, product in zip(inverses, products)]
    return inverses


def local_forms(query, key, trans, beta):
    row, col = iotas(PIECE, PIECE)
    eye = jnp.where(row == col, 1.0, 0.0)
    unit = trans * lax.rsqrt(jnp.sum(trans * trans, axis=-1, keepdims=True) + 1e-06)
    beta_unit = unit * beta
    pieces = [slice(p * PIECE, (p + 1) * PIECE) for p in range(PIECES)]
    units = [unit[p] for p in pieces]
    beta_units = [beta_unit[p] for p in pieces]
    queries = [query[p] for p in pieces]
    keys = [key[p] for p in pieces]
    products = [
        dot(jnp.concatenate([b, q], axis=0), jnp.concatenate([u, k], axis=0), 1, 1)
        for b, q, u, k in zip(beta_units, queries, units, keys)
    ]
    lowers = [jnp.where(row > col, x[:PIECE, :PIECE], 0.0) for x in products]
    beta_keys = [jnp.where(row > col, x[:PIECE, PIECE:], 0.0) for x in products]
    query_dirs = [jnp.where(row >= col, x[PIECE:, :PIECE], 0.0) for x in products]
    inverses = unit_lower_inverses(lowers)
    solved = [dot(i, jnp.concatenate([bk, bu], axis=1)) for i, bk, bu in zip(inverses, beta_keys, beta_units)]
    taken = [dot(d, s) for d, s in zip(query_dirs, solved)]
    own_scores = [x[PIECE:, PIECE:] - y[:, :PIECE] for x, y in zip(products, taken)]
    query_hats = [q - y[:, PIECE:] for q, y in zip(queries, taken)]
    backs = [dot(s, u, 0, 0) for s, u in zip(solved, units)]
    key_hats = [k - z[:PIECE] for k, z in zip(keys, backs)]
    steps_t = [eye - z[PIECE:] for z in backs]
    return query_hats, key_hats, own_scores, steps_t


def kernel(
    n,
    q_hbm, k_hbm, v_hbm, t_hbm, beta_ref, doc_ref, w_hbm,
    out_ref,
    q_in, k_in, t_in, v_in, flat, cols, doc_own,
    scores, ks_send, q_send,
    v_all, ks_all, q_all, doc_all,
    own_o, own_m, own_l,
    cross_o, cross_st, ret_o, ret_st,
    att, att_got, w_own, w_got,
    in_sem, v_ssem, v_rsem, ks_ssem, ks_rsem, q_ssem, q_rsem, d_ssem, d_rsem,
    vz_ssem, kz_ssem, dz_ssem, o_ssem, o_rsem, s_ssem, s_rsem, w_sem, a_sem,
):
    me = lax.axis_index("ctx")
    core = lax.axis_index("head")
    x = lax.rem(me, G)
    row_start = me - x
    up = lax.rem(me + G, n)
    down = lax.rem(me + n - G, n)
    half = ROWS // 2

    def ring(off):
        return lax.rem(x + off, G)

    def remote(src, dst, ssem, rsem, ctx=None, head=None):
        device = {"ctx": me if ctx is None else ctx, "head": core if head is None else head}
        return pltpu.make_async_remote_copy(
            src_ref=src, dst_ref=dst, send_sem=ssem, recv_sem=rsem, device_id=device, device_id_type=MESH
        )

    def head_cols(h):
        return pl.ds(pl.multiple_of(h * DH, DH), DH)

    def load(i, src, dst, h):
        return pltpu.make_async_copy(src.at[:, head_cols(h)], dst.at[h], in_sem.at[i, h])

    loads = ((k_hbm, k_in), (t_hbm, t_in), (q_hbm, q_in), (v_hbm, v_in))
    for off in (3, 2, 1, 0):
        for i in range(3):
            load(i, *loads[i], ring(off)).start()
    for off in (0, 1, 2, 3):
        load(3, *loads[3], ring(off)).start()
    own_w = pltpu.make_async_copy(w_hbm, w_own, w_sem.at[0])

    barrier = pltpu.get_barrier_semaphore()
    for off in (1, 2, 3):
        pl.semaphore_signal(barrier, inc=1, device_id={"ctx": row_start + ring(off), "head": core}, device_id_type=MESH)
    for ctx in (up, down):
        pl.semaphore_signal(barrier, inc=1, device_id={"ctx": ctx, "head": core}, device_id_type=MESH)
    pl.semaphore_signal(barrier, inc=1, device_id={"ctx": me, "head": 1 - core}, device_id_type=MESH)
    pl.semaphore_wait(barrier, 6)

    def v_copy(off):
        h = ring(off)
        return remote(v_hbm.at[:, head_cols(h)], v_all.at[3 + x], v_ssem.at[off], v_rsem.at[3 + x], row_start + h)

    def doc_copy(off):
        return remote(doc_own, doc_all.at[3 + x], d_ssem.at[off], d_rsem.at[3 + x], row_start + ring(off))

    def ks_copy(off):
        h = ring(off)
        return remote(ks_send.at[h], ks_all.at[3 + x], ks_ssem.at[off], ks_rsem.at[3 + x], row_start + h)

    def q_copy(off):
        h = ring(off)
        return remote(q_send.at[h], q_all.at[x], q_ssem.at[off], q_rsem.at[x], row_start + h)

    def from_slot(ref, ssem, rsem, slot):
        return remote(ref.at[slot], ref.at[slot], ssem.at[0], rsem.at[slot], row_start)

    def up_copy(ref, ssem, rsem, b):
        return remote(ref.at[3 + b], ref.at[b - 1], ssem.at[b - 1], rsem.at[b - 1], up)

    w_copy = remote(w_hbm, w_got, w_sem.at[1], w_sem.at[2], None, 1 - core)
    for off in (2, 1, 3):
        v_copy(off).start()
    own_w.start()
    w_copy.start()

    doc_row = doc_ref[...].astype(jnp.float32)
    doc_own[...] = jnp.broadcast_to(doc_row, (8, ROWS))
    flat[...] = jnp.zeros_like(flat)
    flat[0:G, :] = beta_ref[...]
    flat[8:16, :] = jnp.broadcast_to(doc_row, (8, ROWS))
    cols[...] = jnp.transpose(flat[...])
    doc_all[pl.ds(3 + x, 1)] = jnp.broadcast_to(doc_row, (8, ROWS))[None]
    for off in (1, 2, 3):
        doc_copy(off).start()

    lane = lax.broadcasted_iota(jnp.int32, (ROWS, DH), 1)

    @pl.loop(0, G)
    def _(it):
        off = G - 1 - it
        h = ring(off)
        for i in range(3):
            load(i, *loads[i], h).wait()
        beta = jnp.sum(jnp.where(lane == h, cols[...], 0.0), axis=1, keepdims=True)
        query = q_in[h] * (math.log2(math.e) / math.sqrt(DH))
        query_hats, key_hats, own_scores, steps_t = local_forms(query, k_in[h], t_in[h], beta)
        carried = key_hats[0]
        prefix_t = steps_t[0]
        q_send[h, 0:PIECE] = query_hats[0]
        scores[h, 0:PIECE, 0:PIECE] = own_scores[0]
        for p in range(1, PIECES):
            here = slice(p * PIECE, (p + 1) * PIECE)
            scores[h, here, 0 : p * PIECE] = dot(query_hats[p], carried, 1, 1)
            scores[h, here, here] = own_scores[p]
            carried = jnp.concatenate([dot(carried, steps_t[p]), key_hats[p]], axis=0)
            q_send[h, here] = dot(query_hats[p], prefix_t, 1, 1)
            prefix_t = dot(prefix_t, steps_t[p])
        ks_send[h, 0:ROWS] = carried
        ks_send[h, ROWS : ROWS + DH] = prefix_t

        @pl.when(it < G - 1)
        def _():
            ks_copy(off).start()
            q_copy(off).start()

    load(3, *loads[3], x).wait()
    v_all[pl.ds(3 + x, 1)] = v_in[pl.ds(x, 1)]
    ks_all[pl.ds(3 + x, 1)] = ks_send[pl.ds(x, 1)]
    q_all[pl.ds(x, 1)] = q_send[pl.ds(x, 1)]

    for b in (3, 2, 1):
        @pl.when(x != b)
        def _():
            from_slot(v_all, v_ssem, v_rsem, 3 + b).wait_recv()
            from_slot(doc_all, d_ssem, d_rsem, 3 + b).wait_recv()
        up_copy(v_all, vz_ssem, v_rsem, b).start()
        up_copy(doc_all, dz_ssem, d_rsem, b).start()
    for b in (3, 2, 1):
        @pl.when(x != b)
        def _():
            from_slot(ks_all, ks_ssem, ks_rsem, 3 + b).wait_recv()
        up_copy(ks_all, kz_ssem, ks_rsem, b).start()

    for off in (1, 2, 3):
        load(3, *loads[3], ring(off)).wait()
    row, col = iotas(PIECE, PIECE)

    @pl.loop(0, G)
    def _(h):
        for p in range(PIECES):
            here = slice(p * PIECE, (p + 1) * PIECE)
            width = (p + 1) * PIECE
            raw = scores[h, here, 0:width]
            same = cols[here, 8:9] == doc_own[0:1, 0:width]
            wide_row, wide_col = iotas(PIECE, width)
            allowed = same & (wide_row + p * PIECE >= wide_col)
            masked = jnp.where(allowed, raw, MASKED)
            peak = jnp.max(masked, axis=-1, keepdims=True)
            weights = jnp.exp2(masked - peak)
            own_m[h, here] = peak
            own_l[h, here] = jnp.sum(weights, axis=-1, keepdims=True)
            own_o[h, here] = dot(weights, v_in[h, 0:width])

    b0 = (0,)
    @pl.when(x != 0)
    def _():
        from_slot(v_all, v_ssem, v_rsem, 3).wait_recv()
        from_slot(doc_all, d_ssem, d_rsem, 3).wait_recv()
        from_slot(ks_all, ks_ssem, ks_rsem, 3).wait_recv()

    def o_copy(b, slot):
        return remote(cross_o.at[b], ret_o.at[slot], o_ssem.at[b], o_rsem.at[slot], row_start + b)

    def st_copy(b, slot):
        return remote(cross_st.at[b], ret_st.at[slot], s_ssem.at[b], s_rsem.at[slot], row_start + b)

    for b in (3, 2, 1, 0):
        slot = 3 + b

        @pl.when(x != b)
        def _():
            from_slot(q_all, q_ssem, q_rsem, b).wait_recv()

        if b < 3:
            halo = b
            up_copy(v_all, vz_ssem, v_rsem, halo + 1).wait_recv()
            up_copy(doc_all, dz_ssem, d_rsem, halo + 1).wait_recv()
            up_copy(ks_all, kz_ssem, ks_rsem, halo + 1).wait_recv()
        flat[0:8, :] = doc_all[slot]
        doc_col = jnp.transpose(flat[...])[:, 0:1]
        key_docs = []
        for d in (1, 2, 3):
            key_doc = doc_all[slot - d, 0:1, :]
            if slot - d < 3:
                key_doc = jnp.where(me >= G, key_doc, -1.0)
            key_docs.append(key_doc)
        current = q_all[b]
        raws = []
        for d in (1, 2, 3):
            if d > 1:
                current = dot(current, ks_all[slot - d + 1, ROWS : ROWS + DH], 1, 1)
            raw = dot(current, ks_all[slot - d, 0:ROWS], 1, 1)
            raws.append(jnp.where(doc_col == key_docs[d - 1], raw, MASKED))
        peak = functools.reduce(jnp.maximum, [jnp.max(r, axis=-1, keepdims=True) for r in raws])
        total = jnp.zeros((ROWS, 1), jnp.float32)
        summed = jnp.zeros((ROWS, DH), jnp.float32)
        for d in (1, 2, 3):
            weights = jnp.exp2(raws[d - 1] - peak)
            total = total + jnp.sum(weights, axis=-1, keepdims=True)
            summed = summed + dot(weights, v_all[slot - d])
        cross_o[b] = summed
        stats = jnp.where(lane == 0, peak, jnp.where(lane == 1, total, 0.0))
        cross_st[b] = jnp.transpose(stats)[0:8, :]

        @pl.when(x != b)
        def _():
            o_copy(b, x).start()
            st_copy(b, x).start()

        @pl.when(x == b)
        def _():
            ret_o[pl.ds(x, 1)] = cross_o[b][None]
            ret_st[pl.ds(x, 1)] = cross_st[b][None]

    for off in (1, 2, 3):
        h = ring(off)
        remote(ret_o.at[h], ret_o.at[h], o_ssem.at[0], o_rsem.at[h], row_start).wait_recv()
        remote(ret_st.at[h], ret_st.at[h], s_ssem.at[0], s_rsem.at[h], row_start).wait_recv()
    for h in range(G):
        flat[8 * h : 8 * h + 8, :] = ret_st[h]
    stat_cols = jnp.transpose(flat[...])
    for h in range(G):
        other_m = stat_cols[:, 8 * h : 8 * h + 1]
        other_l = stat_cols[:, 8 * h + 1 : 8 * h + 2]
        peak = jnp.maximum(own_m[h], other_m)
        mine = jnp.exp2(own_m[h] - peak)
        other = jnp.exp2(other_m - peak)
        total = mine * own_l[h] + other * other_l
        att[:, h * DH : (h + 1) * DH] = (mine * own_o[h] + other * ret_o[h]) / total

    mine_rows = pl.ds(pl.multiple_of(core * half, half), half)
    other_rows = pl.ds(pl.multiple_of((1 - core) * half, half), half)
    a_copy = remote(att.at[other_rows], att_got, a_sem.at[0], a_sem.at[1], None, 1 - core)
    a_copy.start()
    own_w.wait()
    tile = 512
    for j in range(4):
        at = slice(j * tile, (j + 1) * tile)
        out_ref[:, at] = dot(att[mine_rows, :], w_own[:, at])
    w_copy.wait()
    a_copy.wait()
    for j in range(4):
        at = slice(j * tile, (j + 1) * tile)
        out_ref[:, at] = out_ref[:, at] + dot(att_got[...], w_got[:, at])

    for off in (1, 2, 3):
        v_copy(off).wait_send()
        doc_copy(off).wait_send()
        ks_copy(off).wait_send()
        q_copy(off).wait_send()
    for b in (1, 2, 3):
        up_copy(v_all, vz_ssem, v_rsem, b).wait_send()
        up_copy(doc_all, dz_ssem, d_rsem, b).wait_send()
        up_copy(ks_all, kz_ssem, ks_rsem, b).wait_send()
    for b in range(G):
        @pl.when(x != b)
        def _():
            o_copy(b, x).wait_send()
            st_copy(b, x).wait_send()


def shards(n, queries, keys, values, transitions, betas, documents, out_weight):
    f32 = jnp.float32
    dma = pltpu.SemaphoreType.DMA
    columns = out_weight.shape[1]
    hbm = pl.BlockSpec(memory_space=pl.ANY)
    vmem = pl.BlockSpec(memory_space=pltpu.VMEM)
    heads = pltpu.VMEM((G, ROWS, DH), f32)
    return pl.pallas_call(
        functools.partial(kernel, n),
        out_shape=jax.ShapeDtypeStruct((ROWS // 2, columns), f32),
        in_specs=[hbm, hbm, hbm, hbm, vmem, vmem, hbm],
        out_specs=vmem,
        scratch_shapes=[
            heads, heads, heads, heads,
            pltpu.VMEM((DH, ROWS), f32), pltpu.VMEM((ROWS, DH), f32), pltpu.VMEM((8, ROWS), f32),
            pltpu.VMEM((G, ROWS, ROWS), f32), pltpu.VMEM((G, ROWS + DH, DH), f32), heads,
            pltpu.VMEM((7, ROWS, DH), f32), pltpu.VMEM((7, ROWS + DH, DH), f32), heads, pltpu.VMEM((7, 8, ROWS), f32),
            heads, pltpu.VMEM((G, ROWS, 1), f32), pltpu.VMEM((G, ROWS, 1), f32),
            heads, pltpu.VMEM((G, 8, ROWS), f32), heads, pltpu.VMEM((G, 8, ROWS), f32),
            pltpu.VMEM((ROWS, G * DH), f32), pltpu.VMEM((ROWS // 2, G * DH), f32),
            pltpu.VMEM((G * DH, columns), f32), pltpu.VMEM((G * DH, columns), f32),
            dma((4, G)), dma((4,)), dma((7,)), dma((4,)), dma((7,)), dma((4,)), dma((4,)), dma((4,)), dma((7,)),
            dma((3,)), dma((3,)), dma((3,)), dma((4,)), dma((4,)), dma((4,)), dma((4,)), dma((3,)), dma((2,)),
        ],
        compiler_params=pltpu.CompilerParams(
            collective_id=0, has_side_effects=True, vmem_limit_bytes=60 * 2**20
        ),
        name="path_layer",
    )(queries, keys, values, transitions, betas, documents.reshape(1, ROWS), out_weight)


def solution(mesh):
    return jax.shard_map(
        functools.partial(shards, mesh.shape["ctx"]),
        mesh=mesh,
        in_specs=(
            P("ctx", "head"),
            P("ctx", "head"),
            P("ctx", "head"),
            P("ctx", "head"),
            P("head", "ctx"),
            P("ctx"),
            P("head", None),
        ),
        out_specs=P(("ctx", "head"), None),
        check_vma=False,
    )
```

```python
import functools
import math

import jax
import jax.numpy as jnp
from jax import lax
from jax.experimental import pallas as pl
from jax.experimental.pallas import tpu as pltpu
from jax.sharding import PartitionSpec as P

MESH = pl.DeviceIdType.MESH
HIGH = lax.Precision.HIGH
ROWS = 512
DH = 128
G = 4
PIECE = 128
PIECES = ROWS // PIECE
MASKED = -1e30


def dot(left, right, left_dim=1, right_dim=0):
    return lax.dot_general(
        left,
        right,
        (((left_dim,), (right_dim,)), ((), ())),
        precision=HIGH,
        preferred_element_type=jnp.float32,
    )


def split(value):
    high = value.astype(jnp.bfloat16)
    return high, (value - high.astype(jnp.float32)).astype(jnp.bfloat16)


def half_dot(left, right, left_dim=1, right_dim=0):
    return lax.dot_general(
        left, right, (((left_dim,), (right_dim,)), ((), ())), preferred_element_type=jnp.float32
    )


def iotas(rows, columns):
    return (
        lax.broadcasted_iota(jnp.int32, (rows, columns), 0),
        lax.broadcasted_iota(jnp.int32, (rows, columns), 1),
    )


def unit_lower_inverses(lowers):
    row, col = iotas(PIECE, PIECE)
    eye = jnp.where(row == col, 1.0, 0.0)

    def level_part(lower, bit):
        keep = ((row >> (bit + 1)) == (col >> (bit + 1))) & (((row >> bit) & 1) == 1) & (((col >> bit) & 1) == 0)
        return jnp.where(keep, lower, 0.0)

    inverses = [eye - level_part(lower, 0) for lower in lowers]
    for bit in range(1, 7):
        products = [dot(level_part(lower, bit), inverse) for lower, inverse in zip(lowers, inverses)]
        products = [dot(inverse, product) for inverse, product in zip(inverses, products)]
        inverses = [inverse - product for inverse, product in zip(inverses, products)]
    return inverses


def local_forms(query, key, trans, beta):
    row, col = iotas(PIECE, PIECE)
    eye = jnp.where(row == col, 1.0, 0.0)
    unit = trans * lax.rsqrt(jnp.sum(trans * trans, axis=-1, keepdims=True) + 1e-06)
    beta_unit = unit * beta
    pieces = [slice(p * PIECE, (p + 1) * PIECE) for p in range(PIECES)]
    units = [unit[p] for p in pieces]
    beta_units = [beta_unit[p] for p in pieces]
    queries = [query[p] for p in pieces]
    keys = [key[p] for p in pieces]
    products = [
        dot(jnp.concatenate([b, q], axis=0), jnp.concatenate([u, k], axis=0), 1, 1)
        for b, q, u, k in zip(beta_units, queries, units, keys)
    ]
    lowers = [jnp.where(row > col, x[:PIECE, :PIECE], 0.0) for x in products]
    beta_keys = [jnp.where(row > col, x[:PIECE, PIECE:], 0.0) for x in products]
    query_dirs = [jnp.where(row >= col, x[PIECE:, :PIECE], 0.0) for x in products]
    inverses = unit_lower_inverses(lowers)
    solved = [dot(i, jnp.concatenate([bk, bu], axis=1)) for i, bk, bu in zip(inverses, beta_keys, beta_units)]
    taken = [dot(d, s) for d, s in zip(query_dirs, solved)]
    own_scores = [x[PIECE:, PIECE:] - y[:, :PIECE] for x, y in zip(products, taken)]
    query_hats = [q - y[:, PIECE:] for q, y in zip(queries, taken)]
    backs = [dot(s, u, 0, 0) for s, u in zip(solved, units)]
    key_hats = [k - z[:PIECE] for k, z in zip(keys, backs)]
    steps_t = [eye - z[PIECE:] for z in backs]
    return query_hats, key_hats, own_scores, steps_t


def kernel(
    n,
    q_hbm, k_hbm, v_hbm, t_hbm, beta_ref, doc_ref, w_hbm,
    out_ref,
    q_in, k_in, t_in, v_in, flat, cols, doc_own, doc_cols,
    scores, ks_send, q_send,
    v_all, ks_all, q_all, doc_all,
    own_o, own_m, own_l,
    cross_o, cross_st, ret_o, ret_st,
    att, att_got, w_own, w_got, w_high, w_low, kb, vb, qb,
    in_sem, v_ssem, v_rsem, ks_ssem, ks_rsem, q_ssem, q_rsem, d_ssem, d_rsem,
    vz_ssem, kz_ssem, dz_ssem, o_ssem, o_rsem, s_ssem, s_rsem, w_sem, a_sem,
):
    me = lax.axis_index("ctx")
    core = lax.axis_index("head")
    x = lax.rem(me, G)
    row_start = me - x
    up = lax.rem(me + G, n)
    down = lax.rem(me + n - G, n)
    half = ROWS // 2

    def ring(off):
        return lax.rem(x + off, G)

    def remote(src, dst, ssem, rsem, ctx=None, head=None):
        device = {"ctx": me if ctx is None else ctx, "head": core if head is None else head}
        return pltpu.make_async_remote_copy(
            src_ref=src, dst_ref=dst, send_sem=ssem, recv_sem=rsem, device_id=device, device_id_type=MESH
        )

    def head_cols(h):
        return pl.ds(pl.multiple_of(h * DH, DH), DH)

    def load(i, src, dst, h):
        return pltpu.make_async_copy(src.at[:, head_cols(h)], dst.at[h], in_sem.at[i, h])

    loads = ((k_hbm, k_in), (t_hbm, t_in), (q_hbm, q_in), (v_hbm, v_in))
    for off in (3, 2, 1, 0):
        for i in range(3):
            load(i, *loads[i], ring(off)).start()
    for off in (0, 1, 2, 3):
        load(3, *loads[3], ring(off)).start()
    own_w = pltpu.make_async_copy(w_hbm, w_own, w_sem.at[0])

    doc_row = doc_ref[...].astype(jnp.float32)
    doc_own[...] = jnp.broadcast_to(doc_row, (8, ROWS))
    doc_all[pl.ds(3 + x, 1)] = jnp.broadcast_to(doc_row, (8, ROWS))[None]
    flat[...] = jnp.zeros_like(flat)
    flat[0:G, :] = beta_ref[...]
    barrier = pltpu.get_barrier_semaphore()
    for off in (1, 2, 3):
        pl.semaphore_signal(barrier, inc=1, device_id={"ctx": row_start + ring(off), "head": core}, device_id_type=MESH)
    for ctx in (up, down):
        pl.semaphore_signal(barrier, inc=1, device_id={"ctx": ctx, "head": core}, device_id_type=MESH)
    pl.semaphore_signal(barrier, inc=1, device_id={"ctx": me, "head": 1 - core}, device_id_type=MESH)
    cols[...] = jnp.transpose(flat[...])
    doc_cols[G] = jnp.transpose(jnp.broadcast_to(doc_row, (DH, ROWS)))
    pl.semaphore_wait(barrier, 6)

    def v_copy(off):
        h = ring(off)
        return remote(v_hbm.at[:, head_cols(h)], v_all.at[3 + x], v_ssem.at[off], v_rsem.at[3 + x], row_start + h)

    def doc_copy(off):
        return remote(doc_own, doc_all.at[3 + x], d_ssem.at[off], d_rsem.at[3 + x], row_start + ring(off))

    def ks_copy(off):
        h = ring(off)
        return remote(ks_send.at[h], ks_all.at[3 + x], ks_ssem.at[off], ks_rsem.at[3 + x], row_start + h)

    def q_copy(off):
        h = ring(off)
        return remote(q_send.at[h], q_all.at[x], q_ssem.at[off], q_rsem.at[x], row_start + h)

    def from_slot(ref, ssem, rsem, slot):
        return remote(ref.at[slot], ref.at[slot], ssem.at[0], rsem.at[slot], row_start)

    def up_copy(ref, ssem, rsem, b):
        return remote(ref.at[3 + b], ref.at[b - 1], ssem.at[b - 1], rsem.at[b - 1], up)

    def own_v_up(b):
        return remote(v_hbm.at[:, head_cols(b)], v_all.at[b - 1], vz_ssem.at[b - 1], v_rsem.at[b - 1], up)

    def row_wait(b):
        from_slot(v_all, v_ssem, v_rsem, 3 + b).wait_recv()
        from_slot(doc_all, d_ssem, d_rsem, 3 + b).wait_recv()

    def row_up(b):
        up_copy(v_all, vz_ssem, v_rsem, b).start()
        up_copy(doc_all, dz_ssem, d_rsem, b).start()

    w_copy = remote(w_hbm, w_got, w_sem.at[1], w_sem.at[2], None, 1 - core)
    for off in (1, 3, 2):
        v_copy(off).start()
        doc_copy(off).start()
    for b in (3, 2, 1):
        @pl.when(x == b)
        def _():
            own_v_up(b).start()
            up_copy(doc_all, dz_ssem, d_rsem, b).start()
    own_w.start()
    w_copy.start()

    lane = lax.broadcasted_iota(jnp.int32, (ROWS, DH), 1)

    @pl.loop(0, G)
    def _(it):
        off = G - 1 - it
        h = ring(off)
        for i in range(3):
            load(i, *loads[i], h).wait()
        beta = jnp.sum(jnp.where(lane == h, cols[...], 0.0), axis=1, keepdims=True)
        query = q_in[h] * (math.log2(math.e) / math.sqrt(DH))
        query_hats, key_hats, own_scores, steps_t = local_forms(query, k_in[h], t_in[h], beta)
        carried = key_hats[0]
        prefix_t = steps_t[0]
        q_send[h, 0:PIECE] = query_hats[0]
        scores[h, 0:PIECE, 0:PIECE] = own_scores[0]
        for p in range(1, PIECES):
            here = slice(p * PIECE, (p + 1) * PIECE)
            scores[h, here, 0 : p * PIECE] = dot(query_hats[p], carried, 1, 1)
            scores[h, here, here] = own_scores[p]
            carried = jnp.concatenate([dot(carried, steps_t[p]), key_hats[p]], axis=0)
            q_send[h, here] = dot(query_hats[p], prefix_t, 1, 1)
            prefix_t = dot(prefix_t, steps_t[p])
        ks_send[h, 0:ROWS] = carried
        ks_send[h, ROWS : ROWS + DH] = prefix_t

        @pl.when(it < G - 1)
        def _():
            ks_copy(off).start()

        for step, phases in ((1, (1, 3)), (2, (2,))):
            for b in (3, 2, 1):
                @pl.when((it == step) & functools.reduce(lambda m, c: m | c, [lax.rem(x + G - b, G) == f for f in phases]))
                def _():
                    row_wait(b)
                    row_up(b)

    for off in (3, 2, 1):
        q_copy(off).start()

    load(3, *loads[3], x).wait()
    v_all[pl.ds(3 + x, 1)] = v_in[pl.ds(x, 1)]
    ks_all[pl.ds(3 + x, 1)] = ks_send[pl.ds(x, 1)]
    q_all[pl.ds(x, 1)] = q_send[pl.ds(x, 1)]

    for off in (1, 2, 3):
        load(3, *loads[3], ring(off)).wait()

    def own_attention(h):
        for p in range(PIECES):
            here = slice(p * PIECE, (p + 1) * PIECE)
            width = (p + 1) * PIECE
            raw = scores[h, here, 0:width]
            same = jnp.concatenate([doc_cols[G, here, :]] * (p + 1), axis=1) == doc_own[0:1, 0:width]
            wide_row, wide_col = iotas(PIECE, width)
            allowed = same & (wide_row + p * PIECE >= wide_col)
            masked = jnp.where(allowed, raw, MASKED)
            peak = jnp.max(masked, axis=-1, keepdims=True)
            weights = jnp.exp2(masked - peak)
            own_m[h, here] = peak
            own_l[h, here] = jnp.sum(weights, axis=-1, keepdims=True)
            own_o[h, here] = dot(weights, v_in[h, 0:width])

    @pl.loop(0, G)
    def _(h):
        own_attention(h)

    def split_keys(slot):
        high, low = split(ks_all[slot, 0:ROWS])
        kb[slot] = jnp.concatenate([high, high, low], axis=1)

    def split_values(slot):
        high, low = split(v_all[slot])
        vb[slot] = jnp.concatenate([high, low], axis=1)

    def split_docs(b):
        doc_cols[b] = jnp.transpose(jnp.broadcast_to(doc_all[3 + b, 0:1, :], (DH, ROWS)))

    def ks_wait(b):
        from_slot(ks_all, ks_ssem, ks_rsem, 3 + b).wait_recv()

    for b in (3, 2, 1, 0):
        @pl.when(x != b)
        def _():
            ks_wait(b)
        if b > 0:
            up_copy(ks_all, kz_ssem, ks_rsem, b).start()
        else:
            @pl.when(x != b)
            def _():
                row_wait(0)
        if b < 3:
            split_keys(3 + b)
            split_values(3 + b)
        split_docs(b)

    depth = G * DH
    own_w.wait()
    w_copy.wait_recv()

    @pl.loop(0, 2 * depth // PIECE)
    def _(i):
        at = pl.ds(pl.multiple_of(lax.rem(i, G) * PIECE, PIECE), PIECE)
        to = pl.ds(pl.multiple_of(i * PIECE, PIECE), PIECE)

        @pl.when(i < G)
        def _():
            w_high[to, :], w_low[to, :] = split(w_own[at, :])

        @pl.when(i >= G)
        def _():
            w_high[to, :], w_low[to, :] = split(w_got[at, :])

    def o_copy(b, slot):
        return remote(cross_o.at[b], ret_o.at[slot], o_ssem.at[b], o_rsem.at[slot], row_start + b)

    def st_copy(b, slot):
        return remote(cross_st.at[b], ret_st.at[slot], s_ssem.at[b], s_rsem.at[slot], row_start + b)

    for b in (3, 2, 1, 0):
        slot = 3 + b

        @pl.when(x != b)
        def _():
            from_slot(q_all, q_ssem, q_rsem, b).wait_recv()

        if b < 3:
            halo = b
            up_copy(v_all, vz_ssem, v_rsem, halo + 1).wait_recv()
            up_copy(doc_all, dz_ssem, d_rsem, halo + 1).wait_recv()
            split_values(halo)
            up_copy(ks_all, kz_ssem, ks_rsem, halo + 1).wait_recv()
            split_keys(halo)
        key_docs = []
        current = q_all[b]
        for d in (1, 2, 3):
            key_doc = doc_all[slot - d, 0:1, :]
            if slot - d < 3:
                key_doc = jnp.where(me >= G, key_doc, -1.0)
            key_docs.append(key_doc)
            if d > 1:
                current = dot(current, ks_all[slot - d + 1, ROWS : ROWS + DH], 1, 1)
            high, low = split(current)
            qb[d - 1] = jnp.concatenate([high, low, high], axis=1)
        chunk = ROWS // 2
        for start in (0, chunk):
            here = slice(start, start + chunk)
            doc_col = jnp.concatenate([doc_cols[b, here, :]] * (ROWS // DH), axis=1)
            raws = [
                jnp.where(doc_col == key_docs[d - 1], half_dot(qb[d - 1, here], kb[slot - d], 1, 1), MASKED)
                for d in (1, 2, 3)
            ]
            peak = functools.reduce(jnp.maximum, [jnp.max(r, axis=-1, keepdims=True) for r in raws])
            total = jnp.zeros((chunk, 1), jnp.float32)
            summed = jnp.zeros((chunk, DH), jnp.float32)
            for d in (1, 2, 3):
                weights = jnp.exp2(raws[d - 1] - peak)
                total = total + jnp.sum(weights, axis=-1, keepdims=True)
                high, low = split(weights)
                both = half_dot(high, vb[slot - d])
                summed = summed + both[:, :DH] + both[:, DH:] + half_dot(low, vb[slot - d, :, 0:DH])
            cross_o[b, here] = summed
            stats = jnp.where(lane[:chunk] == 0, peak, jnp.where(lane[:chunk] == 1, total, 0.0))
            cross_st[b, :, here] = jnp.transpose(stats)[0:8, :]

        @pl.when(x != b)
        def _():
            o_copy(b, x).start()
            st_copy(b, x).start()

        @pl.when(x == b)
        def _():
            ret_o[pl.ds(x, 1)] = cross_o[b][None]
            ret_st[pl.ds(x, 1)] = cross_st[b][None]

    for off in (1, 2, 3):
        h = ring(off)
        remote(ret_o.at[h], ret_o.at[h], o_ssem.at[0], o_rsem.at[h], row_start).wait_recv()
        remote(ret_st.at[h], ret_st.at[h], s_ssem.at[0], s_rsem.at[h], row_start).wait_recv()
    for h in range(G):
        flat[8 * h : 8 * h + 8, :] = ret_st[h]
    stat_cols = jnp.transpose(flat[...])
    for h in range(G):
        other_m = stat_cols[:, 8 * h : 8 * h + 1]
        other_l = stat_cols[:, 8 * h + 1 : 8 * h + 2]
        peak = jnp.maximum(own_m[h], other_m)
        mine = jnp.exp2(own_m[h] - peak)
        other = jnp.exp2(other_m - peak)
        total = mine * own_l[h] + other * other_l
        att[:, h * DH : (h + 1) * DH] = (mine * own_o[h] + other * ret_o[h]) / total

    mine_rows = pl.ds(pl.multiple_of(core * half, half), half)
    other_rows = pl.ds(pl.multiple_of((1 - core) * half, half), half)
    a_copy = remote(att.at[other_rows], att_got, a_sem.at[0], a_sem.at[1], None, 1 - core)
    a_copy.start()
    tile = 512
    for part in range(2):
        if part == 1:
            a_copy.wait()
        high, low = split(att[mine_rows, :] if part == 0 else att_got[...])
        both = jnp.concatenate([high, low], axis=1)
        rows = slice(part * depth, (part + 1) * depth)
        for j in range(4):
            at = slice(j * tile, (j + 1) * tile)
            weight = w_high[rows, at]
            term = half_dot(both, jnp.concatenate([weight, weight], axis=0)) + half_dot(high, w_low[rows, at])
            out_ref[:, at] = term if part == 0 else out_ref[:, at] + term

    w_copy.wait_send()
    for off in (1, 2, 3):
        v_copy(off).wait_send()
        doc_copy(off).wait_send()
        ks_copy(off).wait_send()
        q_copy(off).wait_send()
    for b in (1, 2, 3):
        up_copy(v_all, vz_ssem, v_rsem, b).wait_send()
        up_copy(doc_all, dz_ssem, d_rsem, b).wait_send()
        up_copy(ks_all, kz_ssem, ks_rsem, b).wait_send()
    for b in range(G):
        @pl.when(x != b)
        def _():
            o_copy(b, x).wait_send()
            st_copy(b, x).wait_send()


def shards(n, queries, keys, values, transitions, betas, documents, out_weight):
    f32 = jnp.float32
    dma = pltpu.SemaphoreType.DMA
    columns = out_weight.shape[1]
    hbm = pl.BlockSpec(memory_space=pl.ANY)
    vmem = pl.BlockSpec(memory_space=pltpu.VMEM)
    heads = pltpu.VMEM((G, ROWS, DH), f32)
    return pl.pallas_call(
        functools.partial(kernel, n),
        out_shape=jax.ShapeDtypeStruct((ROWS // 2, columns), f32),
        in_specs=[hbm, hbm, hbm, hbm, vmem, vmem, hbm],
        out_specs=vmem,
        scratch_shapes=[
            heads, heads, heads, heads,
            pltpu.VMEM((DH, ROWS), f32), pltpu.VMEM((ROWS, DH), f32), pltpu.VMEM((8, ROWS), f32),
            pltpu.VMEM((G + 1, ROWS, DH), f32),
            pltpu.VMEM((G, ROWS, ROWS), f32), pltpu.VMEM((G, ROWS + DH, DH), f32), heads,
            pltpu.VMEM((7, ROWS, DH), f32), pltpu.VMEM((7, ROWS + DH, DH), f32), heads, pltpu.VMEM((7, 8, ROWS), f32),
            heads, pltpu.VMEM((G, ROWS, 1), f32), pltpu.VMEM((G, ROWS, 1), f32),
            heads, pltpu.VMEM((G, 8, ROWS), f32), heads, pltpu.VMEM((G, 8, ROWS), f32),
            pltpu.VMEM((ROWS, G * DH), f32), pltpu.VMEM((ROWS // 2, G * DH), f32),
            pltpu.VMEM((G * DH, columns), f32), pltpu.VMEM((G * DH, columns), f32),
            pltpu.VMEM((2 * G * DH, columns), jnp.bfloat16), pltpu.VMEM((2 * G * DH, columns), jnp.bfloat16),
            pltpu.VMEM((7, ROWS, 3 * DH), jnp.bfloat16), pltpu.VMEM((7, ROWS, 2 * DH), jnp.bfloat16),
            pltpu.VMEM((3, ROWS, 3 * DH), jnp.bfloat16),
            dma((4, G)), dma((4,)), dma((7,)), dma((4,)), dma((7,)), dma((4,)), dma((4,)), dma((4,)), dma((7,)),
            dma((3,)), dma((3,)), dma((3,)), dma((4,)), dma((4,)), dma((4,)), dma((4,)), dma((3,)), dma((2,)),
        ],
        compiler_params=pltpu.CompilerParams(
            collective_id=0, has_side_effects=True, vmem_limit_bytes=60 * 2**20
        ),
        name="path_layer",
    )(queries, keys, values, transitions, betas, documents.reshape(1, ROWS), out_weight)


def solution(mesh):
    return jax.shard_map(
        functools.partial(shards, mesh.shape["ctx"]),
        mesh=mesh,
        in_specs=(
            P("ctx", "head"),
            P("ctx", "head"),
            P("ctx", "head"),
            P("ctx", "head"),
            P("head", "ctx"),
            P("ctx"),
            P("head", None),
        ),
        out_specs=P(("ctx", "head"), None),
        check_vma=False,
    )
```

```python
import functools
import math

import jax
import jax.numpy as jnp
from jax import lax
from jax.experimental import pallas as pl
from jax.experimental.pallas import tpu as pltpu
from jax.sharding import PartitionSpec as P

MESH = pl.DeviceIdType.MESH
HIGH = lax.Precision.HIGH
ROWS = 512
DH = 128
G = 4
PIECE = 128
PIECES = ROWS // PIECE
MASKED = -1e30
ORDER = ((3, 3, 3, 3), (2, 2, 2, 2), (1, 1, 1, 1), (0, 0, 0, 0))
HALOS = ((), (2,), (1,), (0,))


def dot(left, right, left_dim=1, right_dim=0):
    return lax.dot_general(
        left,
        right,
        (((left_dim,), (right_dim,)), ((), ())),
        precision=HIGH,
        preferred_element_type=jnp.float32,
    )


def split(value):
    high = value.astype(jnp.bfloat16)
    return high, (value - high.astype(jnp.float32)).astype(jnp.bfloat16)


def half_dot(left, right, left_dim=1, right_dim=0):
    return lax.dot_general(
        left, right, (((left_dim,), (right_dim,)), ((), ())), preferred_element_type=jnp.float32
    )


def iotas(rows, columns):
    return (
        lax.broadcasted_iota(jnp.int32, (rows, columns), 0),
        lax.broadcasted_iota(jnp.int32, (rows, columns), 1),
    )


def unit_lower_inverses(lowers):
    row, col = iotas(PIECE, PIECE)
    eye = jnp.where(row == col, 1.0, 0.0)

    def level_part(lower, bit):
        keep = ((row >> (bit + 1)) == (col >> (bit + 1))) & (((row >> bit) & 1) == 1) & (((col >> bit) & 1) == 0)
        return jnp.where(keep, lower, 0.0)

    inverses = [eye - level_part(lower, 0) for lower in lowers]
    for bit in range(1, 7):
        products = [dot(level_part(lower, bit), inverse) for lower, inverse in zip(lowers, inverses)]
        products = [dot(inverse, product) for inverse, product in zip(inverses, products)]
        inverses = [inverse - product for inverse, product in zip(inverses, products)]
    return inverses


def local_forms(query, key, trans, beta):
    row, col = iotas(PIECE, PIECE)
    eye = jnp.where(row == col, 1.0, 0.0)
    unit = trans * lax.rsqrt(jnp.sum(trans * trans, axis=-1, keepdims=True) + 1e-06)
    beta_unit = unit * beta
    pieces = [slice(p * PIECE, (p + 1) * PIECE) for p in range(PIECES)]
    units = [unit[p] for p in pieces]
    beta_units = [beta_unit[p] for p in pieces]
    queries = [query[p] for p in pieces]
    keys = [key[p] for p in pieces]
    products = [
        dot(jnp.concatenate([b, q], axis=0), jnp.concatenate([u, k], axis=0), 1, 1)
        for b, q, u, k in zip(beta_units, queries, units, keys)
    ]
    lowers = [jnp.where(row > col, x[:PIECE, :PIECE], 0.0) for x in products]
    beta_keys = [jnp.where(row > col, x[:PIECE, PIECE:], 0.0) for x in products]
    query_dirs = [jnp.where(row >= col, x[PIECE:, :PIECE], 0.0) for x in products]
    inverses = unit_lower_inverses(lowers)
    solved = [dot(i, jnp.concatenate([bk, bu], axis=1)) for i, bk, bu in zip(inverses, beta_keys, beta_units)]
    taken = [dot(d, s) for d, s in zip(query_dirs, solved)]
    own_scores = [x[PIECE:, PIECE:] - y[:, :PIECE] for x, y in zip(products, taken)]
    query_hats = [q - y[:, PIECE:] for q, y in zip(queries, taken)]
    backs = [dot(s, u, 0, 0) for s, u in zip(solved, units)]
    key_hats = [k - z[:PIECE] for k, z in zip(keys, backs)]
    steps_t = [eye - z[PIECE:] for z in backs]
    return query_hats, key_hats, own_scores, steps_t


def kernel(
    n,
    q_hbm, k_hbm, v_hbm, t_hbm, beta_ref, doc_ref, w_hbm,
    out_ref,
    q_in, k_in, t_in, v_in, flat, cols, doc_own, doc_cols,
    scores, ks_send, q_send,
    v_all, ks_all, q_all, doc_all,
    own_o, own_st,
    cross_o, cross_st, ret_o, ret_st,
    att, att_got, w_own, w_got, w_high, w_low, kb, vb, qb,
    in_sem, v_ssem, v_rsem, ks_ssem, ks_rsem, q_ssem, q_rsem, d_ssem, d_rsem,
    vz_ssem, kz_ssem, dz_ssem, o_ssem, o_rsem, s_ssem, s_rsem, w_sem, a_ssem, a_rsem,
):
    me = lax.axis_index("ctx")
    core = lax.axis_index("head")
    x = lax.rem(me, G)
    row_start = me - x
    up = lax.rem(me + G, n)
    down = lax.rem(me + n - G, n)
    half = ROWS // 2

    def ring(off):
        return lax.rem(x + off, G)

    def remote(src, dst, ssem, rsem, ctx=None, head=None):
        device = {"ctx": me if ctx is None else ctx, "head": core if head is None else head}
        return pltpu.make_async_remote_copy(
            src_ref=src, dst_ref=dst, send_sem=ssem, recv_sem=rsem, device_id=device, device_id_type=MESH
        )

    def head_cols(h):
        return pl.ds(pl.multiple_of(h * DH, DH), DH)

    def load(i, src, dst, h):
        return pltpu.make_async_copy(src.at[:, head_cols(h)], dst.at[h], in_sem.at[i, h])

    loads = ((k_hbm, k_in), (t_hbm, t_in), (q_hbm, q_in), (v_hbm, v_in))
    for off in (3, 2, 1, 0):
        for i in range(3):
            load(i, *loads[i], ring(off)).start()
    for off in (0, 1, 2, 3):
        load(3, *loads[3], ring(off)).start()
    own_w = pltpu.make_async_copy(w_hbm, w_own, w_sem.at[0])

    doc_row = doc_ref[...].astype(jnp.float32)
    doc_own[...] = jnp.broadcast_to(doc_row, (8, ROWS))
    doc_all[pl.ds(3 + x, 1)] = jnp.broadcast_to(doc_row, (8, ROWS))[None]
    flat[...] = jnp.zeros_like(flat)
    flat[0:G, :] = beta_ref[...]
    barrier = pltpu.get_barrier_semaphore()
    for off in (1, 2, 3):
        pl.semaphore_signal(barrier, inc=1, device_id={"ctx": row_start + ring(off), "head": core}, device_id_type=MESH)
    for ctx in (up, down):
        pl.semaphore_signal(barrier, inc=1, device_id={"ctx": ctx, "head": core}, device_id_type=MESH)
    pl.semaphore_signal(barrier, inc=1, device_id={"ctx": me, "head": 1 - core}, device_id_type=MESH)
    cols[...] = jnp.transpose(flat[...])
    doc_cols[G] = jnp.transpose(jnp.broadcast_to(doc_row, (DH, ROWS)))
    pl.semaphore_wait(barrier, 6)

    def v_copy(off):
        h = ring(off)
        return remote(v_hbm.at[:, head_cols(h)], v_all.at[3 + x], v_ssem.at[off], v_rsem.at[3 + x], row_start + h)

    def doc_copy(off):
        return remote(doc_own, doc_all.at[3 + x], d_ssem.at[off], d_rsem.at[3 + x], row_start + ring(off))

    def ks_copy(off):
        h = ring(off)
        return remote(ks_send.at[h], ks_all.at[3 + x], ks_ssem.at[off], ks_rsem.at[3 + x], row_start + h)

    def q_copy(off):
        h = ring(off)
        return remote(q_send.at[h], q_all.at[x], q_ssem.at[off], q_rsem.at[x], row_start + h)

    def from_slot(ref, ssem, rsem, slot):
        return remote(ref.at[slot], ref.at[slot], ssem.at[0], rsem.at[slot], row_start)

    def ks_up(b):
        rows = slice(0, ROWS if b == 1 else ROWS + DH)
        return remote(ks_all.at[3 + b, rows], ks_all.at[b - 1, rows], kz_ssem.at[b - 1], ks_rsem.at[b - 1], up)

    def up_copy(ref, ssem, rsem, b):
        return remote(ref.at[3 + b], ref.at[b - 1], ssem.at[b - 1], rsem.at[b - 1], up)

    def own_v_up(b):
        return remote(v_hbm.at[:, head_cols(b)], v_all.at[b - 1], vz_ssem.at[b - 1], v_rsem.at[b - 1], up)

    def row_wait(b):
        from_slot(v_all, v_ssem, v_rsem, 3 + b).wait_recv()
        from_slot(doc_all, d_ssem, d_rsem, 3 + b).wait_recv()

    def row_up(b):
        up_copy(v_all, vz_ssem, v_rsem, b).start()
        up_copy(doc_all, dz_ssem, d_rsem, b).start()

    w_copy = remote(w_hbm, w_got, w_sem.at[1], w_sem.at[2], None, 1 - core)
    for off in (1, 3):
        v_copy(off).start()
    for off in (1, 3, 2):
        doc_copy(off).start()
    for b in (3, 2, 1):
        @pl.when(x == b)
        def _():
            own_v_up(b).start()
            up_copy(doc_all, dz_ssem, d_rsem, b).start()
    own_w.start()
    w_copy.start()

    lane = lax.broadcasted_iota(jnp.int32, (ROWS, DH), 1)

    @pl.loop(0, G)
    def _(it):
        off = G - 1 - it
        h = ring(off)
        for i in range(3):
            load(i, *loads[i], h).wait()
        beta = jnp.sum(jnp.where(lane == h, cols[...], 0.0), axis=1, keepdims=True)
        query = q_in[h] * (math.log2(math.e) / math.sqrt(DH))
        query_hats, key_hats, own_scores, steps_t = local_forms(query, k_in[h], t_in[h], beta)
        carried = key_hats[0]
        prefix_t = steps_t[0]
        q_send[h, 0:PIECE] = query_hats[0]
        scores[h, 0:PIECE, 0:PIECE] = own_scores[0]
        for p in range(1, PIECES):
            here = slice(p * PIECE, (p + 1) * PIECE)
            scores[h, here, 0 : p * PIECE] = dot(query_hats[p], carried, 1, 1)
            scores[h, here, here] = own_scores[p]
            carried = jnp.concatenate([dot(carried, steps_t[p]), key_hats[p]], axis=0)
            q_send[h, here] = dot(query_hats[p], prefix_t, 1, 1)
            prefix_t = dot(prefix_t, steps_t[p])
        ks_send[h, 0:ROWS] = carried
        ks_send[h, ROWS : ROWS + DH] = prefix_t

        @pl.when(it < G - 1)
        def _():
            ks_copy(off).start()

        @pl.when(it == 0)
        def _():
            v_copy(2).start()

        for step, phases in ((1, (1, 3)), (2, (2,))):
            for b in (3, 2, 1):
                @pl.when((it == step) & functools.reduce(lambda m, c: m | c, [lax.rem(x + G - b, G) == f for f in phases]))
                def _():
                    row_wait(b)
                    row_up(b)

    for off in (3, 2, 1):
        q_copy(off).start()

    load(3, *loads[3], x).wait()
    v_all[pl.ds(3 + x, 1)] = v_in[pl.ds(x, 1)]
    ks_all[pl.ds(3 + x, 1)] = ks_send[pl.ds(x, 1)]
    q_all[pl.ds(x, 1)] = q_send[pl.ds(x, 1)]

    for off in (1, 2, 3):
        load(3, *loads[3], ring(off)).wait()

    def own_attention(h):
        for p in range(PIECES):
            here = slice(p * PIECE, (p + 1) * PIECE)
            width = (p + 1) * PIECE
            raw = scores[h, here, 0:width]
            same = jnp.concatenate([doc_cols[G, here, :]] * (p + 1), axis=1) == doc_own[0:1, 0:width]
            wide_row, wide_col = iotas(PIECE, width)
            allowed = same & (wide_row + p * PIECE >= wide_col)
            masked = jnp.where(allowed, raw, MASKED)
            peak = jnp.max(masked, axis=-1, keepdims=True)
            weights = jnp.exp2(masked - peak)
            total = jnp.sum(weights, axis=-1, keepdims=True)
            stats = jnp.where(lane[:PIECE] == 0, peak, jnp.where(lane[:PIECE] == 1, total, 0.0))
            own_st[h, :, here] = jnp.transpose(stats)[0:8, :]
            own_o[h, here] = dot(weights, v_in[h, 0:width])

    @pl.loop(0, G)
    def _(h):
        own_attention(h)

    def split_keys(slot):
        high, low = split(ks_all[slot, 0:ROWS])
        kb[slot] = jnp.concatenate([high, high, low], axis=1)

    def split_values(slot):
        high, low = split(v_all[slot])
        vb[slot] = jnp.concatenate([high, low], axis=1)

    def split_docs(b):
        doc_cols[b] = jnp.transpose(jnp.broadcast_to(doc_all[3 + b, 0:1, :], (DH, ROWS)))

    def ks_wait(b):
        from_slot(ks_all, ks_ssem, ks_rsem, 3 + b).wait_recv()

    for b in (3, 2, 1, 0):
        @pl.when(x != b)
        def _():
            ks_wait(b)
        if b > 0:
            ks_up(b).start()
        else:
            @pl.when(x != b)
            def _():
                row_wait(0)
        if b < 3:
            split_keys(3 + b)
            split_values(3 + b)
        split_docs(b)

    depth = G * DH
    own_w.wait()
    w_copy.wait_recv()

    @pl.loop(0, 2 * depth // PIECE)
    def _(i):
        at = pl.ds(pl.multiple_of(lax.rem(i, G) * PIECE, PIECE), PIECE)
        to = pl.ds(pl.multiple_of(i * PIECE, PIECE), PIECE)

        @pl.when(i < G)
        def _():
            w_high[to, :], w_low[to, :] = split(w_own[at, :])

        @pl.when(i >= G)
        def _():
            w_high[to, :], w_low[to, :] = split(w_got[at, :])

    def o_copy(b, part):
        rows = slice(part * half, (part + 1) * half)
        return remote(
            cross_o.at[b, rows], ret_o.at[x, rows], o_ssem.at[b, part], o_rsem.at[x, part], row_start + b
        )

    def st_copy(b):
        return remote(cross_st.at[b], ret_st.at[x], s_ssem.at[b], s_rsem.at[x], row_start + b)

    for turn, order in enumerate(ORDER):
        table = sum(b << (2 * i) for i, b in enumerate(order))
        b = (table >> (2 * x)) & 3
        place = 3 + b

        @pl.when(x != b)
        def _():
            from_slot(q_all, q_ssem, q_rsem, b).wait_recv()

        for halo in HALOS[turn]:
            up_copy(v_all, vz_ssem, v_rsem, halo + 1).wait_recv()
            up_copy(doc_all, dz_ssem, d_rsem, halo + 1).wait_recv()
            ks_up(halo + 1).wait_recv()
            split_values(halo)
            split_keys(halo)

        key_docs = []
        current = q_all[b]
        for d in (1, 2, 3):
            slot = place - d
            exists = (slot >= 3) | (me >= G)
            key_docs.append(jnp.where(exists, doc_all[slot, 0:1, :], -1.0))
            if d > 1:
                current = dot(current, ks_all[slot + 1, ROWS : ROWS + DH], 1, 1)
            high, low = split(current)
            qb[d - 1] = jnp.concatenate([high, low, high], axis=1)
        chunk = ROWS // 2
        for start in (0, chunk):
            here = slice(start, start + chunk)
            doc_col = jnp.concatenate([doc_cols[b, here, :]] * (ROWS // DH), axis=1)
            raws = [
                jnp.where(doc_col == key_docs[d - 1], half_dot(qb[d - 1, here], kb[place - d], 1, 1), MASKED)
                for d in (1, 2, 3)
            ]
            peak = functools.reduce(jnp.maximum, [jnp.max(r, axis=-1, keepdims=True) for r in raws])
            total = jnp.zeros((chunk, 1), jnp.float32)
            summed = jnp.zeros((chunk, DH), jnp.float32)
            for d in (1, 2, 3):
                weights = jnp.exp2(raws[d - 1] - peak)
                total = total + jnp.sum(weights, axis=-1, keepdims=True)
                high, low = split(weights)
                both = half_dot(high, vb[place - d])
                summed = summed + both[:, :DH] + both[:, DH:] + half_dot(low, vb[place - d, :, 0:DH])
            cross_o[b, here] = summed

            @pl.when(x != b)
            def _():
                o_copy(b, start // chunk).start()

            stats = jnp.where(lane[:chunk] == 0, peak, jnp.where(lane[:chunk] == 1, total, 0.0))
            cross_st[b, :, here] = jnp.transpose(stats)[0:8, :]

        @pl.when(x != b)
        def _():
            st_copy(b).start()

        @pl.when(x == b)
        def _():
            ret_o[pl.ds(x, 1)] = cross_o[pl.ds(b, 1)]
            ret_st[pl.ds(x, 1)] = cross_st[pl.ds(b, 1)]

    mine_rows = pl.ds(pl.multiple_of(core * half, half), half)
    other_rows = pl.ds(pl.multiple_of((1 - core) * half, half), half)

    def a_copy(h):
        return remote(att.at[h, other_rows], att_got.at[h], a_ssem.at[h], a_rsem.at[h], None, 1 - core)

    def wide(row_values):
        return jnp.transpose(jnp.broadcast_to(row_values, (DH, ROWS)))

    def join(h):
        own_m, own_l = own_st[h, 0:1, :], own_st[h, 1:2, :]
        other_m, other_l = ret_st[h, 0:1, :], ret_st[h, 1:2, :]
        peak = jnp.maximum(own_m, other_m)
        mine = jnp.exp2(own_m - peak)
        other = jnp.exp2(other_m - peak)
        total = mine * own_l + other * other_l
        att[h] = wide(mine / total) * own_o[h] + wide(other / total) * ret_o[h]
        a_copy(h).start()

    def project(parts, add):
        pairs = [split(rows) for rows, _ in parts]
        lefts = [jnp.concatenate([high, low], axis=1) for high, low in pairs]
        both = jnp.concatenate(lefts, axis=1)
        highs = jnp.concatenate([high for high, _ in pairs], axis=1)
        tile = 512
        for j in range(4):
            at = slice(j * tile, (j + 1) * tile)
            weights = [w_high[pl.ds(begin, DH), at] for _, begin in parts]
            lows = [w_low[pl.ds(begin, DH), at] for _, begin in parts]
            doubled = jnp.concatenate([w for weight in weights for w in (weight, weight)], axis=0)
            term = half_dot(both, doubled) + half_dot(highs, jnp.concatenate(lows, axis=0))
            out_ref[:, at] = out_ref[:, at] + term if add else term

    def begin(h, mine):
        return pl.multiple_of(h * DH + (0 if mine else depth), DH)

    for group in ((0, 1, 3, 2),):
        heads = [ring(off) for off in group]
        for h, off in zip(heads, group):
            if off > 0:
                for part in range(2):
                    rows = slice(part * half, (part + 1) * half)
                    remote(
                        ret_o.at[h, rows], ret_o.at[h, rows], o_ssem.at[0, part], o_rsem.at[h, part], row_start
                    ).wait_recv()
                remote(ret_st.at[h], ret_st.at[h], s_ssem.at[0], s_rsem.at[h], row_start).wait_recv()
            join(h)
        project([(att[h, mine_rows, :], begin(h, True)) for h in heads], False)
        for h in heads:
            a_copy(h).wait_recv()
        project([(att_got[h], begin(h, False)) for h in heads], True)

    w_copy.wait_send()
    for off in (1, 2, 3):
        v_copy(off).wait_send()
        doc_copy(off).wait_send()
        ks_copy(off).wait_send()
        q_copy(off).wait_send()
    for b in (1, 2, 3):
        up_copy(v_all, vz_ssem, v_rsem, b).wait_send()
        up_copy(doc_all, dz_ssem, d_rsem, b).wait_send()
        ks_up(b).wait_send()
    for b in range(G):
        @pl.when(x != b)
        def _():
            o_copy(b, 0).wait_send()
            o_copy(b, 1).wait_send()
            st_copy(b).wait_send()

    for h in range(G):
        a_copy(h).wait_send()


def shards(n, queries, keys, values, transitions, betas, documents, out_weight):
    f32 = jnp.float32
    dma = pltpu.SemaphoreType.DMA
    columns = out_weight.shape[1]
    hbm = pl.BlockSpec(memory_space=pl.ANY)
    vmem = pl.BlockSpec(memory_space=pltpu.VMEM)
    heads = pltpu.VMEM((G, ROWS, DH), f32)
    return pl.pallas_call(
        functools.partial(kernel, n),
        out_shape=jax.ShapeDtypeStruct((ROWS // 2, columns), f32),
        in_specs=[hbm, hbm, hbm, hbm, vmem, vmem, hbm],
        out_specs=vmem,
        scratch_shapes=[
            heads, heads, heads, heads,
            pltpu.VMEM((DH, ROWS), f32), pltpu.VMEM((ROWS, DH), f32), pltpu.VMEM((8, ROWS), f32),
            pltpu.VMEM((G + 1, ROWS, DH), f32),
            pltpu.VMEM((G, ROWS, ROWS), f32), pltpu.VMEM((G, ROWS + DH, DH), f32), heads,
            pltpu.VMEM((7, ROWS, DH), f32), pltpu.VMEM((7, ROWS + DH, DH), f32), heads, pltpu.VMEM((7, 8, ROWS), f32),
            heads, pltpu.VMEM((G, 8, ROWS), f32),
            heads, pltpu.VMEM((G, 8, ROWS), f32), heads, pltpu.VMEM((G, 8, ROWS), f32),
            heads, pltpu.VMEM((G, ROWS // 2, DH), f32),
            pltpu.VMEM((G * DH, columns), f32), pltpu.VMEM((G * DH, columns), f32),
            pltpu.VMEM((2 * G * DH, columns), jnp.bfloat16), pltpu.VMEM((2 * G * DH, columns), jnp.bfloat16),
            pltpu.VMEM((7, ROWS, 3 * DH), jnp.bfloat16), pltpu.VMEM((7, ROWS, 2 * DH), jnp.bfloat16),
            pltpu.VMEM((3, ROWS, 3 * DH), jnp.bfloat16),
            dma((4, G)), dma((4,)), dma((7,)), dma((4,)), dma((7,)), dma((4,)), dma((4,)), dma((4,)), dma((7,)),
            dma((3,)), dma((3,)), dma((3,)), dma((4, 2)), dma((4, 2)), dma((4,)), dma((4,)), dma((3,)), dma((4,)), dma((4,)),
        ],
        compiler_params=pltpu.CompilerParams(
            collective_id=0, has_side_effects=True, vmem_limit_bytes=60 * 2**20
        ),
        name="path_layer",
    )(queries, keys, values, transitions, betas, documents.reshape(1, ROWS), out_weight)


def solution(mesh):
    return jax.shard_map(
        functools.partial(shards, mesh.shape["ctx"]),
        mesh=mesh,
        in_specs=(
            P("ctx", "head"),
            P("ctx", "head"),
            P("ctx", "head"),
            P("ctx", "head"),
            P("head", "ctx"),
            P("ctx"),
            P("head", None),
        ),
        out_specs=P(("ctx", "head"), None),
        check_vma=False,
    )
```

```python
import functools
import math

import jax
import jax.numpy as jnp
from jax import lax
from jax.experimental import pallas as pl
from jax.experimental.pallas import tpu as pltpu
from jax.sharding import PartitionSpec as P

MESH = pl.DeviceIdType.MESH
HIGH = lax.Precision.HIGH
ROWS = 512
DH = 128
G = 4
PIECE = 128
PIECES = ROWS // PIECE
MASKED = -1e30
ORDER = ((3, 3, 3, 3), (2, 2, 2, 2), (1, 1, 1, 1), (0, 0, 0, 0))
HALOS = ((), (2,), (1,), (0,))


def dot(left, right, left_dim=1, right_dim=0):
    return lax.dot_general(
        left,
        right,
        (((left_dim,), (right_dim,)), ((), ())),
        precision=HIGH,
        preferred_element_type=jnp.float32,
    )


def split(value):
    high = value.astype(jnp.bfloat16)
    return high, (value - high.astype(jnp.float32)).astype(jnp.bfloat16)


def half_dot(left, right, left_dim=1, right_dim=0):
    return lax.dot_general(
        left, right, (((left_dim,), (right_dim,)), ((), ())), preferred_element_type=jnp.float32
    )


def iotas(rows, columns):
    return (
        lax.broadcasted_iota(jnp.int32, (rows, columns), 0),
        lax.broadcasted_iota(jnp.int32, (rows, columns), 1),
    )


def unit_lower_inverses(lowers):
    row, col = iotas(PIECE, PIECE)
    eye = jnp.where(row == col, 1.0, 0.0)

    def level_part(lower, bit):
        keep = ((row >> (bit + 1)) == (col >> (bit + 1))) & (((row >> bit) & 1) == 1) & (((col >> bit) & 1) == 0)
        return jnp.where(keep, lower, 0.0)

    inverses = [eye - level_part(lower, 0) for lower in lowers]
    for bit in range(1, 7):
        products = [dot(level_part(lower, bit), inverse) for lower, inverse in zip(lowers, inverses)]
        products = [dot(inverse, product) for inverse, product in zip(inverses, products)]
        inverses = [inverse - product for inverse, product in zip(inverses, products)]
    return inverses


def local_forms(query, key, trans, beta):
    row, col = iotas(PIECE, PIECE)
    eye = jnp.where(row == col, 1.0, 0.0)
    unit = trans * lax.rsqrt(jnp.sum(trans * trans, axis=-1, keepdims=True) + 1e-06)
    beta_unit = unit * beta
    pieces = [slice(p * PIECE, (p + 1) * PIECE) for p in range(PIECES)]
    units = [unit[p] for p in pieces]
    beta_units = [beta_unit[p] for p in pieces]
    queries = [query[p] for p in pieces]
    keys = [key[p] for p in pieces]
    products = [
        dot(jnp.concatenate([b, q], axis=0), jnp.concatenate([u, k], axis=0), 1, 1)
        for b, q, u, k in zip(beta_units, queries, units, keys)
    ]
    lowers = [jnp.where(row > col, x[:PIECE, :PIECE], 0.0) for x in products]
    beta_keys = [jnp.where(row > col, x[:PIECE, PIECE:], 0.0) for x in products]
    query_dirs = [jnp.where(row >= col, x[PIECE:, :PIECE], 0.0) for x in products]
    inverses = unit_lower_inverses(lowers)
    solved = [dot(i, jnp.concatenate([bk, bu], axis=1)) for i, bk, bu in zip(inverses, beta_keys, beta_units)]
    taken = [dot(d, s) for d, s in zip(query_dirs, solved)]
    own_scores = [x[PIECE:, PIECE:] - y[:, :PIECE] for x, y in zip(products, taken)]
    query_hats = [q - y[:, PIECE:] for q, y in zip(queries, taken)]
    backs = [dot(s, u, 0, 0) for s, u in zip(solved, units)]
    key_hats = [k - z[:PIECE] for k, z in zip(keys, backs)]
    steps_t = [eye - z[PIECE:] for z in backs]
    return query_hats, key_hats, own_scores, steps_t


def kernel(
    n,
    q_hbm, k_hbm, v_hbm, t_hbm, beta_ref, doc_ref, w_hbm,
    out_ref,
    q_in, k_in, t_in, v_in, flat, cols, doc_own, doc_cols,
    scores, ks_send, q_send,
    v_all, ks_all, q_all, doc_all,
    own_o, own_st,
    cross_o, cross_st, ret_o, ret_st,
    att, att_got, w_own, w_got, w_high, w_low, kb, vb, qb,
    in_sem, v_ssem, v_rsem, ks_ssem, ks_rsem, q_ssem, q_rsem, d_ssem, d_rsem,
    vz_ssem, kz_ssem, dz_ssem, o_ssem, o_rsem, s_ssem, s_rsem, w_sem, a_ssem, a_rsem,
):
    me = lax.axis_index("ctx")
    core = lax.axis_index("head")
    x = lax.rem(me, G)
    row_start = me - x
    up = lax.rem(me + G, n)
    down = lax.rem(me + n - G, n)
    half = ROWS // 2

    def ring(off):
        return lax.rem(x + off, G)

    def remote(src, dst, ssem, rsem, ctx=None, head=None):
        device = {"ctx": me if ctx is None else ctx, "head": core if head is None else head}
        return pltpu.make_async_remote_copy(
            src_ref=src, dst_ref=dst, send_sem=ssem, recv_sem=rsem, device_id=device, device_id_type=MESH
        )

    def head_cols(h):
        return pl.ds(pl.multiple_of(h * DH, DH), DH)

    def load(i, src, dst, h):
        return pltpu.make_async_copy(src.at[:, head_cols(h)], dst.at[h], in_sem.at[i, h])

    loads = ((k_hbm, k_in), (t_hbm, t_in), (q_hbm, q_in), (v_hbm, v_in))
    for off in (3, 2, 1, 0):
        for i in range(3):
            load(i, *loads[i], ring(off)).start()
    for off in (0, 1, 2, 3):
        load(3, *loads[3], ring(off)).start()
    own_w = pltpu.make_async_copy(w_hbm, w_own, w_sem.at[0])

    doc_row = doc_ref[...].astype(jnp.float32)
    doc_own[...] = jnp.broadcast_to(doc_row, (8, ROWS))
    doc_all[pl.ds(3 + x, 1)] = jnp.broadcast_to(doc_row, (8, ROWS))[None]
    flat[...] = jnp.zeros_like(flat)
    flat[0:G, :] = beta_ref[...]
    barrier = pltpu.get_barrier_semaphore()
    for off in (1, 2, 3):
        pl.semaphore_signal(barrier, inc=1, device_id={"ctx": row_start + ring(off), "head": core}, device_id_type=MESH)
    for ctx in (up, down):
        pl.semaphore_signal(barrier, inc=1, device_id={"ctx": ctx, "head": core}, device_id_type=MESH)
    pl.semaphore_signal(barrier, inc=1, device_id={"ctx": me, "head": 1 - core}, device_id_type=MESH)
    cols[...] = jnp.transpose(flat[...])
    doc_cols[G] = jnp.transpose(jnp.broadcast_to(doc_row, (DH, ROWS)))
    pl.semaphore_wait(barrier, 6)

    def v_copy(off):
        h = ring(off)
        return remote(v_hbm.at[:, head_cols(h)], v_all.at[3 + x], v_ssem.at[off], v_rsem.at[3 + x], row_start + h)

    def doc_copy(off):
        return remote(doc_own, doc_all.at[3 + x], d_ssem.at[off], d_rsem.at[3 + x], row_start + ring(off))

    def ks_copy(off):
        h = ring(off)
        return remote(ks_send.at[h], ks_all.at[3 + x], ks_ssem.at[off], ks_rsem.at[3 + x], row_start + h)

    def q_copy(off):
        h = ring(off)
        return remote(q_send.at[h], q_all.at[x], q_ssem.at[off], q_rsem.at[x], row_start + h)

    def from_slot(ref, ssem, rsem, slot):
        return remote(ref.at[slot], ref.at[slot], ssem.at[0], rsem.at[slot], row_start)

    def ks_up(b):
        rows = slice(0, ROWS if b == 1 else ROWS + DH)
        return remote(ks_all.at[3 + b, rows], ks_all.at[b - 1, rows], kz_ssem.at[b - 1], ks_rsem.at[b - 1], up)

    def up_copy(ref, ssem, rsem, b):
        return remote(ref.at[3 + b], ref.at[b - 1], ssem.at[b - 1], rsem.at[b - 1], up)

    def own_v_up(b):
        return remote(v_hbm.at[:, head_cols(b)], v_all.at[b - 1], vz_ssem.at[b - 1], v_rsem.at[b - 1], up)

    def row_wait(b):
        from_slot(v_all, v_ssem, v_rsem, 3 + b).wait_recv()
        from_slot(doc_all, d_ssem, d_rsem, 3 + b).wait_recv()

    def row_up(b):
        up_copy(v_all, vz_ssem, v_rsem, b).start()
        up_copy(doc_all, dz_ssem, d_rsem, b).start()

    w_copy = remote(w_hbm, w_got, w_sem.at[1], w_sem.at[2], None, 1 - core)
    for off in (1, 3):
        v_copy(off).start()
    for off in (1, 3, 2):
        doc_copy(off).start()
    for b in (3, 2, 1):
        @pl.when(x == b)
        def _():
            own_v_up(b).start()
            up_copy(doc_all, dz_ssem, d_rsem, b).start()
    own_w.start()
    w_copy.start()

    lane = lax.broadcasted_iota(jnp.int32, (ROWS, DH), 1)

    @pl.loop(0, G)
    def _(it):
        off = G - 1 - it
        h = ring(off)
        for i in range(3):
            load(i, *loads[i], h).wait()
        beta = jnp.sum(jnp.where(lane == h, cols[...], 0.0), axis=1, keepdims=True)
        query = q_in[h] * (math.log2(math.e) / math.sqrt(DH))
        query_hats, key_hats, own_scores, steps_t = local_forms(query, k_in[h], t_in[h], beta)
        carried = key_hats[0]
        prefix_t = steps_t[0]
        q_send[h, 0:PIECE] = query_hats[0]
        scores[h, 0:PIECE, 0:PIECE] = own_scores[0]
        for p in range(1, PIECES):
            here = slice(p * PIECE, (p + 1) * PIECE)
            scores[h, here, 0 : p * PIECE] = dot(query_hats[p], carried, 1, 1)
            scores[h, here, here] = own_scores[p]
            carried = jnp.concatenate([dot(carried, steps_t[p]), key_hats[p]], axis=0)
            q_send[h, here] = dot(query_hats[p], prefix_t, 1, 1)
            prefix_t = dot(prefix_t, steps_t[p])
        ks_send[h, 0:ROWS] = carried
        ks_send[h, ROWS : ROWS + DH] = prefix_t

        @pl.when(it < G - 1)
        def _():
            ks_copy(off).start()

        @pl.when(it == 0)
        def _():
            v_copy(2).start()

        for step, phases in ((1, (1, 3)), (2, (2,))):
            for b in (3, 2, 1):
                @pl.when((it == step) & functools.reduce(lambda m, c: m | c, [lax.rem(x + G - b, G) == f for f in phases]))
                def _():
                    row_wait(b)
                    row_up(b)

    for off in (3, 2, 1):
        q_copy(off).start()

    load(3, *loads[3], x).wait()
    v_all[pl.ds(3 + x, 1)] = v_in[pl.ds(x, 1)]
    ks_all[pl.ds(3 + x, 1)] = ks_send[pl.ds(x, 1)]
    q_all[pl.ds(x, 1)] = q_send[pl.ds(x, 1)]

    for off in (1, 2, 3):
        load(3, *loads[3], ring(off)).wait()

    def own_attention(h):
        for p in range(PIECES):
            here = slice(p * PIECE, (p + 1) * PIECE)
            width = (p + 1) * PIECE
            raw = scores[h, here, 0:width]
            same = jnp.concatenate([doc_cols[G, here, :]] * (p + 1), axis=1) == doc_own[0:1, 0:width]
            wide_row, wide_col = iotas(PIECE, width)
            allowed = same & (wide_row + p * PIECE >= wide_col)
            masked = jnp.where(allowed, raw, MASKED)
            peak = jnp.max(masked, axis=-1, keepdims=True)
            weights = jnp.exp2(masked - peak)
            total = jnp.sum(weights, axis=-1, keepdims=True)
            stats = jnp.where(lane[:PIECE] == 0, peak, jnp.where(lane[:PIECE] == 1, total, 0.0))
            own_st[h, :, here] = jnp.transpose(stats)[0:8, :]
            own_o[h, here] = dot(weights, v_in[h, 0:width])

    @pl.loop(0, G)
    def _(h):
        own_attention(h)

    def split_keys(slot):
        high, low = split(ks_all[slot, 0:ROWS])
        kb[slot] = jnp.concatenate([high, high, low], axis=1)

    def split_values(slot):
        high, low = split(v_all[slot])
        vb[slot] = jnp.concatenate([high, low], axis=1)

    def split_docs(b):
        doc_cols[b] = jnp.transpose(jnp.broadcast_to(doc_all[3 + b, 0:1, :], (DH, ROWS)))

    def ks_wait(b):
        from_slot(ks_all, ks_ssem, ks_rsem, 3 + b).wait_recv()

    for b in (2, 3, 1, 0):
        @pl.when(x != b)
        def _():
            ks_wait(b)
        if b > 0:
            ks_up(b).start()
        else:
            @pl.when(x != b)
            def _():
                row_wait(0)
        if b < 3:
            split_keys(3 + b)
            split_values(3 + b)
        split_docs(b)

    depth = G * DH
    own_w.wait()
    w_copy.wait_recv()

    @pl.loop(0, 2 * depth // PIECE)
    def _(i):
        at = pl.ds(pl.multiple_of(lax.rem(i, G) * PIECE, PIECE), PIECE)
        to = pl.ds(pl.multiple_of(i * PIECE, PIECE), PIECE)

        @pl.when(i < G)
        def _():
            w_high[to, :], w_low[to, :] = split(w_own[at, :])

        @pl.when(i >= G)
        def _():
            w_high[to, :], w_low[to, :] = split(w_got[at, :])

    def o_copy(b, part):
        rows = slice(part * half, (part + 1) * half)
        return remote(
            cross_o.at[b, rows], ret_o.at[x, rows], o_ssem.at[b, part], o_rsem.at[x, part], row_start + b
        )

    def st_copy(b):
        return remote(cross_st.at[b], ret_st.at[x], s_ssem.at[b], s_rsem.at[x], row_start + b)

    for turn, order in enumerate(ORDER):
        table = sum(b << (2 * i) for i, b in enumerate(order))
        b = (table >> (2 * x)) & 3
        place = 3 + b

        @pl.when(x != b)
        def _():
            from_slot(q_all, q_ssem, q_rsem, b).wait_recv()

        for halo in HALOS[turn]:
            up_copy(v_all, vz_ssem, v_rsem, halo + 1).wait_recv()
            up_copy(doc_all, dz_ssem, d_rsem, halo + 1).wait_recv()
            ks_up(halo + 1).wait_recv()
            split_values(halo)
            split_keys(halo)

        key_docs = []
        current = q_all[b]
        for d in (1, 2, 3):
            slot = place - d
            exists = (slot >= 3) | (me >= G)
            key_docs.append(jnp.where(exists, doc_all[slot, 0:1, :], -1.0))
            if d > 1:
                current = dot(current, ks_all[slot + 1, ROWS : ROWS + DH], 1, 1)
            high, low = split(current)
            qb[d - 1] = jnp.concatenate([high, low, high], axis=1)
        chunk = ROWS // 2
        for start in (0, chunk):
            here = slice(start, start + chunk)
            doc_col = jnp.concatenate([doc_cols[b, here, :]] * (ROWS // DH), axis=1)
            raws = [
                jnp.where(doc_col == key_docs[d - 1], half_dot(qb[d - 1, here], kb[place - d], 1, 1), MASKED)
                for d in (1, 2, 3)
            ]
            peak = functools.reduce(jnp.maximum, [jnp.max(r, axis=-1, keepdims=True) for r in raws])
            total = jnp.zeros((chunk, 1), jnp.float32)
            summed = jnp.zeros((chunk, DH), jnp.float32)
            for d in (1, 2, 3):
                weights = jnp.exp2(raws[d - 1] - peak)
                total = total + jnp.sum(weights, axis=-1, keepdims=True)
                high, low = split(weights)
                both = half_dot(high, vb[place - d])
                summed = summed + both[:, :DH] + both[:, DH:] + half_dot(low, vb[place - d, :, 0:DH])
            cross_o[b, here] = summed

            @pl.when(x != b)
            def _():
                o_copy(b, start // chunk).start()

            stats = jnp.where(lane[:chunk] == 0, peak, jnp.where(lane[:chunk] == 1, total, 0.0))
            cross_st[b, :, here] = jnp.transpose(stats)[0:8, :]

        @pl.when(x != b)
        def _():
            st_copy(b).start()

        @pl.when(x == b)
        def _():
            ret_o[pl.ds(x, 1)] = cross_o[pl.ds(b, 1)]
            ret_st[pl.ds(x, 1)] = cross_st[pl.ds(b, 1)]

    mine_rows = pl.ds(pl.multiple_of(core * half, half), half)
    other_rows = pl.ds(pl.multiple_of((1 - core) * half, half), half)

    def a_copy(h):
        return remote(att.at[h, other_rows], att_got.at[h], a_ssem.at[h], a_rsem.at[h], None, 1 - core)

    def wide(row_values):
        return jnp.transpose(jnp.broadcast_to(row_values, (DH, ROWS)))

    def join(h):
        own_m, own_l = own_st[h, 0:1, :], own_st[h, 1:2, :]
        other_m, other_l = ret_st[h, 0:1, :], ret_st[h, 1:2, :]
        peak = jnp.maximum(own_m, other_m)
        mine = jnp.exp2(own_m - peak)
        other = jnp.exp2(other_m - peak)
        total = mine * own_l + other * other_l
        att[h] = wide(mine / total) * own_o[h] + wide(other / total) * ret_o[h]
        a_copy(h).start()

    def project(parts, add):
        pairs = [split(rows) for rows, _ in parts]
        lefts = [jnp.concatenate([high, low], axis=1) for high, low in pairs]
        both = jnp.concatenate(lefts, axis=1)
        highs = jnp.concatenate([high for high, _ in pairs], axis=1)
        tile = 512
        for j in range(4):
            at = slice(j * tile, (j + 1) * tile)
            weights = [w_high[pl.ds(begin, DH), at] for _, begin in parts]
            lows = [w_low[pl.ds(begin, DH), at] for _, begin in parts]
            doubled = jnp.concatenate([w for weight in weights for w in (weight, weight)], axis=0)
            term = half_dot(both, doubled) + half_dot(highs, jnp.concatenate(lows, axis=0))
            out_ref[:, at] = out_ref[:, at] + term if add else term

    def begin(h, mine):
        return pl.multiple_of(h * DH + (0 if mine else depth), DH)

    for group in ((0, 1, 3, 2),):
        heads = [ring(off) for off in group]
        for h, off in zip(heads, group):
            if off > 0:
                for part in range(2):
                    rows = slice(part * half, (part + 1) * half)
                    remote(
                        ret_o.at[h, rows], ret_o.at[h, rows], o_ssem.at[0, part], o_rsem.at[h, part], row_start
                    ).wait_recv()
                remote(ret_st.at[h], ret_st.at[h], s_ssem.at[0], s_rsem.at[h], row_start).wait_recv()
            join(h)
        project([(att[h, mine_rows, :], begin(h, True)) for h in heads], False)
        for h in heads:
            a_copy(h).wait_recv()
        project([(att_got[h], begin(h, False)) for h in heads], True)

    w_copy.wait_send()
    for off in (1, 2, 3):
        v_copy(off).wait_send()
        doc_copy(off).wait_send()
        ks_copy(off).wait_send()
        q_copy(off).wait_send()
    for b in (1, 2, 3):
        up_copy(v_all, vz_ssem, v_rsem, b).wait_send()
        up_copy(doc_all, dz_ssem, d_rsem, b).wait_send()
        ks_up(b).wait_send()
    for b in range(G):
        @pl.when(x != b)
        def _():
            o_copy(b, 0).wait_send()
            o_copy(b, 1).wait_send()
            st_copy(b).wait_send()

    for h in range(G):
        a_copy(h).wait_send()


def shards(n, queries, keys, values, transitions, betas, documents, out_weight):
    f32 = jnp.float32
    dma = pltpu.SemaphoreType.DMA
    columns = out_weight.shape[1]
    hbm = pl.BlockSpec(memory_space=pl.ANY)
    vmem = pl.BlockSpec(memory_space=pltpu.VMEM)
    heads = pltpu.VMEM((G, ROWS, DH), f32)
    return pl.pallas_call(
        functools.partial(kernel, n),
        out_shape=jax.ShapeDtypeStruct((ROWS // 2, columns), f32),
        in_specs=[hbm, hbm, hbm, hbm, vmem, vmem, hbm],
        out_specs=vmem,
        scratch_shapes=[
            heads, heads, heads, heads,
            pltpu.VMEM((DH, ROWS), f32), pltpu.VMEM((ROWS, DH), f32), pltpu.VMEM((8, ROWS), f32),
            pltpu.VMEM((G + 1, ROWS, DH), f32),
            pltpu.VMEM((G, ROWS, ROWS), f32), pltpu.VMEM((G, ROWS + DH, DH), f32), heads,
            pltpu.VMEM((7, ROWS, DH), f32), pltpu.VMEM((7, ROWS + DH, DH), f32), heads, pltpu.VMEM((7, 8, ROWS), f32),
            heads, pltpu.VMEM((G, 8, ROWS), f32),
            heads, pltpu.VMEM((G, 8, ROWS), f32), heads, pltpu.VMEM((G, 8, ROWS), f32),
            heads, pltpu.VMEM((G, ROWS // 2, DH), f32),
            pltpu.VMEM((G * DH, columns), f32), pltpu.VMEM((G * DH, columns), f32),
            pltpu.VMEM((2 * G * DH, columns), jnp.bfloat16), pltpu.VMEM((2 * G * DH, columns), jnp.bfloat16),
            pltpu.VMEM((7, ROWS, 3 * DH), jnp.bfloat16), pltpu.VMEM((7, ROWS, 2 * DH), jnp.bfloat16),
            pltpu.VMEM((3, ROWS, 3 * DH), jnp.bfloat16),
            dma((4, G)), dma((4,)), dma((7,)), dma((4,)), dma((7,)), dma((4,)), dma((4,)), dma((4,)), dma((7,)),
            dma((3,)), dma((3,)), dma((3,)), dma((4, 2)), dma((4, 2)), dma((4,)), dma((4,)), dma((3,)), dma((4,)), dma((4,)),
        ],
        compiler_params=pltpu.CompilerParams(
            collective_id=0, has_side_effects=True, vmem_limit_bytes=60 * 2**20
        ),
        name="path_layer",
    )(queries, keys, values, transitions, betas, documents.reshape(1, ROWS), out_weight)


def solution(mesh):
    return jax.shard_map(
        functools.partial(shards, mesh.shape["ctx"]),
        mesh=mesh,
        in_specs=(
            P("ctx", "head"),
            P("ctx", "head"),
            P("ctx", "head"),
            P("ctx", "head"),
            P("head", "ctx"),
            P("ctx"),
            P("head", None),
        ),
        out_specs=P(("ctx", "head"), None),
        check_vma=False,
    )
```
